256 devices in a mesh: ctx: 64 (over z, x, core), ch: 4 (over y).
Axes of the slice: x: 4, y: 4, z: 8, core: 2. Of those that a mesh axis runs over, the one named last changes fastest.
Arguments:
- signal: bfloat16 [32768, 1024], P('ctx', 'ch'), may hold values from -6 to 6
- gate_v: bfloat16 [32768, 1024], P('ctx', 'ch'), may hold values from -6 to 6
- taps: float32 [32768, 1024], P('ctx', 'ch'), may hold values from -1 to 1
- skip: float32 [1024], P('ch'), may hold values from -1 to 1
- norm_gain: float32 [1024], replicated, may hold values from 0.5 to 1.5
- router: float32 [1024, 32], replicated, may hold values from -0.1875 to 0.1875
- w_up: bfloat16 [64, 1024, 256], P('ctx'), may hold values from -0.1875 to 0.1875
- w_down: bfloat16 [64, 256, 1024], P('ctx'), may hold values from -0.25 to 0.25
- routes: int32 [32768, 2], P(('ctx', 'ch')), may hold values from 0 to 31, all different within a row; in each aligned block of 128 rows (0 to 127, 128 to 255, ...) at most 16 rows name the same one
Outputs:
- mixed: bfloat16 [32768, 1024], P('ctx', 'ch')
- moe_out: bfloat16 [32768, 1024], P('ctx', 'ch')
The draws below stay inside these ranges and needn't reach their ends.
Inputs may be any that keep to these rules, and one draw needn't show every extreme that they name: `routes`: each row names two different experts. In each aligned block of 128 rows no expert is named by more than 16 rows.
All inputs are finite; a program needn't handle non-finite values.
Results may differ from the reference program's by a relative error of at most 0.017.
Values may be sent and summed in bfloat16 or wider, within the bound.
A program may use at most 64 MiB of HBM per device.

```python
import math
import jax
import jax.numpy as jnp
import numpy as np
from jax import lax

D = 1024
HID = 512
EXPERTS = 32
CAP = 16
HALF = 256
PARTS_SIZE = 64
TOKENS = 32768
ROWS_EX = 128


def draw_taps(key, part):
    key_noise, key_rate = jax.random.split(jax.random.fold_in(key, 17))
    steps = jnp.arange(TOKENS, dtype=jnp.float32)[:, None]
    length = jnp.exp(jax.random.uniform(key_rate, (1, D), jnp.float32, math.log(40.0), math.log(4.0 * TOKENS)))
    noise = jax.random.truncated_normal(key_noise, -4.0, 4.0, (TOKENS, D), jnp.float32)
    ratio = jnp.exp(-1.0 / length)
    scale = jnp.sqrt((1.0 - ratio * ratio) / (1.0 - jnp.exp(-2.0 * TOKENS / length)))
    return noise * scale * jnp.exp(-steps / length)


def level_of(rng, dims, shards, least, high):
    gain, own = 1.0, jax.random.fold_in(rng, 6)
    for axis_at, blocks in shards:
        steps = jnp.exp(jax.random.uniform(jax.random.fold_in(own, axis_at), (blocks,), jnp.float32, least / len(shards), high / len(shards)))
        gain = gain * jnp.repeat(steps, dims[axis_at] // blocks).reshape([-1 if axis == axis_at else 1 for axis in range(len(dims))])
    return gain


def assign_block(own_key, own, number, rows, count, top, most, skew):
    sequence = jax.random.permutation(own_key, count)
    packed, common = portions_of(count, rows * top, most, skew, True), portions_of(count, rows * top, most, skew, False)
    places = jnp.arange(count)

    def named(sizes, rotation):
        used = int((sizes > 0).sum())
        fixed = max(1, used // 4)
        shifted = fixed + (places - fixed + rotation * (used - fixed)) % max(1, count - fixed)
        return jnp.zeros((count,), jnp.int32).at[sequence[jnp.where(places < fixed, places, shifted)]].set(jnp.asarray(sizes, jnp.int32))

    sizes = jnp.where(number % 4 == 0, named(packed, number // 4), named(common, number - number // 4 - 1))
    mixed = jax.random.permutation(jax.random.fold_in(own, 3), count)
    donor, sink = mixed[0:count // 2 * 2:2], mixed[1:count // 2 * 2:2]
    room = jnp.minimum(sizes[donor] - 1, most - sizes[sink]) // 2
    room = jnp.where((donor == sequence[0]) | (sink == sequence[0]) | (sizes[sink] == 0), 0, jnp.maximum(room, 0))
    shifted = jax.random.randint(jax.random.fold_in(own, 4), (count // 2,), 0, 1 << 20) % (room + 1)
    sizes = sizes.at[donor].add(-shifted).at[sink].add(shifted)
    members = jnp.searchsorted(jnp.cumsum(sizes), jnp.arange(rows * top), side="right").astype(jnp.int32)
    grid = members.reshape(top, rows).T
    grid = grid[jax.random.permutation(jax.random.fold_in(own, 1), rows)]
    rotation = jax.random.randint(jax.random.fold_in(own, 2), (rows, 1), 0, top)
    return jnp.take_along_axis(grid, (jnp.arange(top)[None, :] + rotation) % top, axis=1)


def portions_of(amount, total, most, slope, full):
    loads = [(1 << 20) // math.isqrt(rank ** slope) + 1 for rank in range(1, amount + 1)]
    largest = most if full else min(most, max(-(-total // amount), total * loads[0] // sum(loads)))
    least = 1 if total - largest >= amount - 1 else 0
    given, surplus = [largest] + [least] * (amount - 1), total - largest - least * (amount - 1)
    while surplus > 0:
        free = [i for i in range(1, amount) if given[i] < largest] or [i for i in range(1, amount) if given[i] < most]
        mass, left = sum([loads[i] for i in free]), surplus
        for i in free:
            extra = min(most - given[i], max(1, left * loads[i] // mass), surplus)
            given[i] = given[i] + extra
            surplus = surplus - extra
    return np.array(given)


def centred(key, dims, spread, reach, cuts=(), kind=jnp.bfloat16):
    result = spread * jax.random.normal(key, dims, jnp.float32)
    if cuts:
        result = result * level_of(key, dims, cuts, -0.22, 0.18)
    return jnp.clip(result, -reach, reach).astype(kind)


def setup_inputs(seed: int = 0) -> dict:
    keys = jax.random.split(jax.random.key(seed), 10)
    signal = centred(keys[0], (TOKENS, D), 1.0, 6.0, ((0, 64), (1, 4)))
    gate_v = centred(keys[1], (TOKENS, D), 1.0, 6.0, ((0, 64), (1, 4)))
    taps = draw_taps(jax.random.fold_in(keys[9], 71), 0)
    skip = jnp.clip(jax.random.uniform(keys[3], (D,), jnp.float32, -1.0, 1.0) * level_of(keys[3], (D,), ((0, 4),), -0.4, 0.0), -1.0, 1.0)
    norm_gain = jnp.clip(1.0 + 0.1 * jax.random.normal(keys[4], (D,), jnp.float32), 0.5, 1.5)
    router = centred(keys[5], (D, EXPERTS), D ** -0.5, 0.1875, (), jnp.float32)
    w_up = centred(keys[6], (PARTS_SIZE, D, HALF), D ** -0.5, 0.1875, ((0, 64),))
    w_down = centred(keys[7], (PARTS_SIZE, HALF, D), HID ** -0.5, 0.25, ((0, 64),))
    routes_keys = jax.random.split(jax.random.fold_in(keys[8], 1), TOKENS // ROWS_EX)
    routes_turns = jax.random.permutation(jax.random.fold_in(keys[8], 3), TOKENS // ROWS_EX)
    routes = jax.vmap(lambda own, number: assign_block(jax.random.fold_in(keys[8], 2), own, number, ROWS_EX, EXPERTS, 2, CAP, 2))(routes_keys, routes_turns).reshape((TOKENS, 2))
    return dict(signal=signal, gate_v=gate_v, taps=taps, skip=skip, norm_gain=norm_gain, router=router, w_up=w_up, w_down=w_down, routes=routes)


def reference(signal, gate_v, taps, skip, norm_gain, router, w_up, w_down, routes):
    total = signal.shape[0]
    width = signal.shape[1]
    sig_float = signal.astype(jnp.float32)
    spec_sig = jnp.fft.rfft(sig_float, n=2 * total, axis=0)
    spec_tap = jnp.fft.rfft(taps, n=2 * total, axis=0)
    conv = jnp.fft.irfft(spec_sig * spec_tap, n=2 * total, axis=0)[:total].astype(jnp.float32)
    mixed = (gate_v.astype(jnp.float32) * (conv + skip * sig_float)).astype(jnp.bfloat16)
    rows_float = mixed.astype(jnp.float32)
    scale_row = lax.rsqrt(lax.optimization_barrier(jnp.mean(rows_float * rows_float, axis=-1, keepdims=True)) + 1e-05)
    normed = (rows_float * scale_row * norm_gain).astype(jnp.bfloat16)
    logits = jnp.dot(normed.astype(jnp.float32), router, precision=lax.Precision.HIGHEST)
    gates = jax.nn.sigmoid(jnp.take_along_axis(logits, routes, axis=1))
    nblock = total // ROWS_EX
    flat = routes.reshape(nblock, 2 * ROWS_EX)
    onehot = (flat[:, :, None] == jnp.arange(EXPERTS, dtype=jnp.int32)[None, None, :]).astype(jnp.int32)
    slot_of = lax.optimization_barrier(jnp.sum((jnp.cumsum(onehot, axis=1) - onehot) * onehot, axis=-1)).astype(jnp.int32)
    token_of = (jnp.arange(total * 2, dtype=jnp.int32) // 2).reshape(nblock, 2 * ROWS_EX)
    target = flat * (nblock * CAP) + jnp.arange(nblock, dtype=jnp.int32)[:, None] * CAP + slot_of
    target = target.reshape(-1).astype(jnp.int32)
    table = jnp.full((EXPERTS * nblock * CAP,), total, jnp.int32).at[target].set(token_of.reshape(-1))
    gate_table = jnp.zeros((EXPERTS * nblock * CAP,), jnp.float32).at[target].set(gates.reshape(-1))
    table = table.reshape(EXPERTS, nblock * CAP)
    gate_table = gate_table.reshape(EXPERTS, nblock * CAP)
    padded = jnp.concatenate([normed, jnp.zeros((1, width), jnp.bfloat16)], axis=0)
    up_pairs = w_up.reshape(EXPERTS, 2, width, HALF)
    down_pairs = w_down.reshape(EXPERTS, 2, HALF, width)

    def expert_step(accum, inputs):
        index_rows, gate_rows, up_pair, down_pair = inputs
        chosen = padded[index_rows]
        summed = jnp.zeros((chosen.shape[0], width), jnp.float32)
        for half in range(2):
            hidden = jax.nn.gelu(jnp.dot(chosen, up_pair[half], preferred_element_type=jnp.float32), approximate=True).astype(jnp.bfloat16)
            part = jnp.dot(hidden, down_pair[half], preferred_element_type=jnp.float32).astype(jnp.bfloat16)
            summed = summed + part.astype(jnp.float32)
        accum = accum.at[index_rows].add(gate_rows[:, None] * summed)
        return (accum, None)
    start = jnp.zeros((total + 1, width), jnp.float32)
    accum, unused = lax.scan(expert_step, start, (table, gate_table, up_pairs, down_pairs))
    moe_out = accum[:total].astype(jnp.bfloat16)
    return (mixed, moe_out)
```

```python
import math

import jax
import jax.numpy as jnp
import numpy as np
from jax import lax
from jax.experimental import pallas as pl
from jax.experimental.pallas import tpu as pltpu
from jax.sharding import PartitionSpec as P

CAP = 16
bf16 = jnp.bfloat16
f32 = jnp.float32


def dft_constants(shards, tok, chans):
    total = shards * tok
    fields = 2 * chans
    row = np.arange(shards)
    col = np.arange(tok)
    outer = 2.0 * np.pi * row[None, :] * (row[:, None] + 0.25) / shards
    first = np.concatenate([np.cos(outer), -np.sin(outer)], axis=0)
    first = np.repeat(first, fields, axis=1)
    last = np.concatenate([np.cos(outer.T), -np.sin(outer.T)], axis=1) / total
    last = np.repeat(last, chans, axis=0)
    turn = 2.0 * np.pi * (row[:, None] + 0.25) * col[None, :] / total
    inner = 2.0 * np.pi * ((col[:, None] * col[None, :]) % tok) / tok
    as16 = lambda a: jnp.asarray(a.astype(np.float32), bf16)
    as32 = lambda a: jnp.asarray(a.astype(np.float32))
    return (
        as16(first),
        as32(np.cos(turn)),
        as32(-np.sin(turn)),
        as16(np.cos(inner)),
        as16(np.sin(inner)),
        as16(last),
    )


def dot(a, b):
    return jnp.dot(a, b, preferred_element_type=f32)


def conv_kernel(shards, chans, r_ref, first_ref, tr_ref, ti_ref, c_ref, s_ref, last_ref, o_ref, re_ref, im_ref):
    fields = 2 * chans
    data = r_ref[...]
    first = first_ref[...]
    lane = lax.broadcasted_iota(jnp.int32, first.shape, 1) % fields
    tr, ti = tr_ref[...], ti_ref[...]
    for field in range(fields):
        g = dot(jnp.where(lane == field, first, jnp.zeros_like(first)), data)
        g_re, g_im = g[:shards], g[shards:]
        rows = pl.ds(field * shards, shards)
        re_ref[rows, :] = (g_re * tr - g_im * ti).astype(bf16)
        im_ref[rows, :] = (g_re * ti + g_im * tr).astype(bf16)
    cos, sin = c_ref[...], s_ref[...]
    re, im = re_ref[...], im_ref[...]
    x_re = dot(re, cos) + dot(im, sin)
    x_im = dot(im, cos) - dot(re, sin)
    half = chans * shards
    p_re = (x_re[:half] * x_re[half:] - x_im[:half] * x_im[half:]).astype(bf16)
    p_im = (x_re[:half] * x_im[half:] + x_im[:half] * x_re[half:]).astype(bf16)
    g_re = dot(p_re, cos) - dot(p_im, sin)
    g_im = dot(p_im, cos) + dot(p_re, sin)
    last = last_ref[...]
    row = lax.broadcasted_iota(jnp.int32, last.shape, 0) % chans
    total = jnp.zeros(o_ref.shape, f32)
    for chan in range(chans):
        rows = slice(chan * shards, (chan + 1) * shards)
        a = (g_re[rows] * tr + g_im[rows] * ti).astype(bf16)
        b = (g_im[rows] * tr - g_re[rows] * ti).astype(bf16)
        both = jnp.concatenate([a, b], axis=0)
        total += dot(jnp.where(row == chan, last, jnp.zeros_like(last)), both)
    o_ref[...] = total.astype(bf16)


def route_kernel(experts, x_ref, gain_ref, router_ref, routes_ref, routes_t_ref, send_ref, hi_ref, lo_ref):
    count = x_ref.shape[0]
    slots = experts * CAP
    x = x_ref[...].astype(f32)
    scale = lax.rsqrt(jnp.mean(x * x, axis=-1, keepdims=True) + 1e-05)
    normed = (x * scale * gain_ref[...]).astype(bf16)
    logits = jnp.dot(
        normed.astype(f32), router_ref[...], precision=lax.Precision.HIGHEST, preferred_element_type=f32
    )
    gates = jax.nn.sigmoid(logits)
    g_hi = gates.astype(bf16)
    g_lo = (gates - g_hi.astype(f32)).astype(bf16)
    ids = lax.broadcasted_iota(jnp.int32, (count, experts), 1)
    routes = routes_ref[...]
    named = ((routes[:, 0:1] == ids) | (routes[:, 1:2] == ids)).astype(f32).astype(bf16)
    rows = lax.broadcasted_iota(jnp.int32, (count, count), 0)
    cols = lax.broadcasted_iota(jnp.int32, (count, count), 1)
    rank = dot((cols < rows).astype(f32).astype(bf16), named).astype(bf16)
    spread = (
        lax.broadcasted_iota(jnp.int32, (experts, slots), 1) // CAP
        == lax.broadcasted_iota(jnp.int32, (experts, slots), 0)
    ).astype(f32).astype(bf16)
    slot = (lax.broadcasted_iota(jnp.int32, (count, slots), 1) % CAP).astype(f32)
    here = (dot(named, spread) > 0.5) & (dot(rank, spread) == slot)
    hi_ref[...] = jnp.where(here, dot(g_hi, spread), 0.0).astype(bf16)
    lo_ref[...] = jnp.where(here, dot(g_lo, spread), 0.0).astype(bf16)
    ids_t = lax.broadcasted_iota(jnp.int32, (experts, count), 0)
    routes_t = routes_t_ref[...]
    named_t = ((routes_t[0:1, :] == ids_t) | (routes_t[1:2, :] == ids_t)).astype(f32).astype(bf16)
    rank_t = dot(named_t, (rows < cols).astype(f32).astype(bf16)).astype(bf16)
    spread_t = (
        lax.broadcasted_iota(jnp.int32, (slots, experts), 0) // CAP
        == lax.broadcasted_iota(jnp.int32, (slots, experts), 1)
    ).astype(f32).astype(bf16)
    slot_t = (lax.broadcasted_iota(jnp.int32, (slots, count), 0) % CAP).astype(f32)
    here_t = (dot(spread_t, named_t) > 0.5) & (dot(spread_t, rank_t) == slot_t)
    send_ref[...] = dot(here_t.astype(f32).astype(bf16), normed).astype(bf16)


def expert_kernel(x_ref, up_ref, down_ref, o_ref):
    hidden = jax.nn.gelu(dot(x_ref[...], up_ref[...]), approximate=True).astype(bf16)
    o_ref[...] = dot(hidden, down_ref[...]).astype(bf16)


def combine_kernel(hi_ref, lo_ref, back_ref, o_ref):
    back = back_ref[...]
    o_ref[...] = (dot(hi_ref[...], back) + dot(lo_ref[...], back)).astype(bf16)


def call(kernel, out_shape, *args, scratch=()):
    return pl.pallas_call(
        kernel,
        out_shape=out_shape,
        in_specs=[pl.BlockSpec(memory_space=pltpu.VMEM)] * len(args),
        out_specs=jax.tree.map(lambda _: pl.BlockSpec(memory_space=pltpu.VMEM), out_shape),
        scratch_shapes=list(scratch),
    )(*args)


def body(signal, gate_v, taps, skip, norm_gain, router, w_up, w_down, routes):
    tok_dev, ch_dev = signal.shape
    shards = lax.axis_size("ctx")
    chans = ch_dev // shards
    experts = router.shape[1]
    width = norm_gain.shape[0]
    shape = jax.ShapeDtypeStruct
    constants = dft_constants(shards, tok_dev, chans)

    sig_t = signal.T.reshape(shards, chans, tok_dev)
    tap_t = taps.astype(bf16).T.reshape(shards, chans, tok_dev)
    packed = jnp.concatenate([sig_t, tap_t], axis=1)
    fields = lax.all_to_all(packed, "ctx", split_axis=0, concat_axis=0, tiled=True)
    conv = call(
        lambda *refs: conv_kernel(shards, chans, *refs),
        shape((shards * chans, tok_dev), bf16),
        fields.reshape(shards * 2 * chans, tok_dev),
        *constants,
        scratch=[pltpu.VMEM((2 * chans * shards, tok_dev), bf16)] * 2,
    )
    conv = lax.all_to_all(
        conv.reshape(shards, chans, tok_dev), "ctx", split_axis=0, concat_axis=0, tiled=True
    )
    conv = conv.reshape(ch_dev, tok_dev).T.astype(f32)
    mixed = (gate_v.astype(f32) * (conv + skip * signal.astype(f32))).astype(bf16)
    full_rows = lax.all_to_all(mixed, "ch", split_axis=0, concat_axis=1, tiled=True)
    slots = experts * CAP
    rows = full_rows.shape[0]
    send, hi, lo = call(
        lambda *refs: route_kernel(experts, *refs),
        (shape((slots, width), bf16), shape((rows, slots), bf16), shape((rows, slots), bf16)),
        full_rows,
        norm_gain[None, :],
        router,
        routes,
        routes.T,
    )
    same_side = [[2 * e + side for e in range(shards // 2)] for side in range(2)]
    swap = [(i, i ^ 1) for i in range(shards)]

    def exchange(block):
        out = lax.all_to_all(
            block.reshape(experts, CAP, width),
            "ctx",
            split_axis=0,
            concat_axis=0,
            axis_index_groups=same_side,
            tiled=True,
        )
        return out.reshape(slots, width)

    mine = exchange(send)
    theirs = lax.ppermute(mine, "ctx", swap)
    up, down = w_up[0], w_down[0]
    out_theirs = call(expert_kernel, shape((slots, width), bf16), theirs, up, down)
    partner_part = lax.ppermute(out_theirs, "ctx", swap)
    out_mine = call(expert_kernel, shape((slots, width), bf16), mine, up, down)
    summed = (out_mine.astype(f32) + partner_part.astype(f32)).astype(bf16)
    back = exchange(summed)
    moe_rows = call(combine_kernel, shape((rows, width), bf16), hi, lo, back)
    moe_out = lax.all_to_all(moe_rows, "ch", split_axis=1, concat_axis=0, tiled=True)
    return (mixed, moe_out)


def solution(mesh):
    in_specs = (
        P("ctx", "ch"),
        P("ctx", "ch"),
        P("ctx", "ch"),
        P("ch"),
        P(),
        P(),
        P("ctx", None, None),
        P("ctx", None, None),
        P(("ctx", "ch"), None),
    )
    out_specs = (P("ctx", "ch"), P("ctx", "ch"))
    return jax.shard_map(body, mesh=mesh, in_specs=in_specs, out_specs=out_specs, check_vma=False)
```

```python
import math

import jax
import jax.numpy as jnp
import numpy as np
from jax import lax
from jax.experimental import pallas as pl
from jax.experimental.pallas import tpu as pltpu
from jax.sharding import PartitionSpec as P

CAP = 16
bf16 = jnp.bfloat16
f32 = jnp.float32


def dft_constants(shards, tok, chans):
    total = shards * tok
    fields = 2 * chans
    row = np.arange(shards)
    col = np.arange(tok)
    outer = 2.0 * np.pi * row[None, :] * (row[:, None] + 0.25) / shards
    first = np.concatenate([np.cos(outer), -np.sin(outer)], axis=0)
    first = np.repeat(first, fields, axis=1)
    last = np.concatenate([np.cos(outer.T), -np.sin(outer.T)], axis=1) / total
    last = np.repeat(last, chans, axis=0)
    turn = 2.0 * np.pi * (row[:, None] + 0.25) * col[None, :] / total
    inner = 2.0 * np.pi * ((col[:, None] * col[None, :]) % tok) / tok
    as16 = lambda a: jnp.asarray(a.astype(np.float32), bf16)
    as32 = lambda a: jnp.asarray(a.astype(np.float32))
    return (
        as16(first),
        as32(np.cos(turn)),
        as32(-np.sin(turn)),
        as16(np.cos(inner)),
        as16(np.sin(inner)),
        as16(last),
    )


def dot(a, b):
    return jnp.dot(a, b, preferred_element_type=f32)


def conv_kernel(shards, chans, r_ref, first_ref, tr_ref, ti_ref, c_ref, s_ref, last_ref, o_ref, re_ref, im_ref):
    fields = 2 * chans
    data = r_ref[...]
    first = first_ref[...]
    lane = lax.broadcasted_iota(jnp.int32, first.shape, 1) % fields
    tr, ti = tr_ref[...], ti_ref[...]
    for field in range(fields):
        g = dot(jnp.where(lane == field, first, jnp.zeros_like(first)), data)
        g_re, g_im = g[:shards], g[shards:]
        rows = pl.ds(field * shards, shards)
        re_ref[rows, :] = (g_re * tr - g_im * ti).astype(bf16)
        im_ref[rows, :] = (g_re * ti + g_im * tr).astype(bf16)
    cos, sin = c_ref[...], s_ref[...]
    re, im = re_ref[...], im_ref[...]
    x_re = dot(re, cos) + dot(im, sin)
    x_im = dot(im, cos) - dot(re, sin)
    half = chans * shards
    p_re = (x_re[:half] * x_re[half:] - x_im[:half] * x_im[half:]).astype(bf16)
    p_im = (x_re[:half] * x_im[half:] + x_im[:half] * x_re[half:]).astype(bf16)
    g_re = dot(p_re, cos) - dot(p_im, sin)
    g_im = dot(p_im, cos) + dot(p_re, sin)
    last = last_ref[...]
    row = lax.broadcasted_iota(jnp.int32, last.shape, 0) % chans
    total = jnp.zeros(o_ref.shape, f32)
    for chan in range(chans):
        rows = slice(chan * shards, (chan + 1) * shards)
        a = (g_re[rows] * tr + g_im[rows] * ti).astype(bf16)
        b = (g_im[rows] * tr - g_re[rows] * ti).astype(bf16)
        both = jnp.concatenate([a, b], axis=0)
        total += dot(jnp.where(row == chan, last, jnp.zeros_like(last)), both)
    o_ref[...] = total.astype(bf16)


def route_kernel(experts, x_ref, gain_ref, router_ref, routes_ref, routes_t_ref, send_ref, hi_ref, lo_ref):
    count = x_ref.shape[0]
    slots = experts * CAP
    x = x_ref[...].astype(f32)
    scale = lax.rsqrt(jnp.mean(x * x, axis=-1, keepdims=True) + 1e-05)
    normed = (x * scale * gain_ref[...]).astype(bf16)
    logits = jnp.dot(
        normed.astype(f32), router_ref[...], precision=lax.Precision.HIGHEST, preferred_element_type=f32
    )
    gates = jax.nn.sigmoid(logits)
    g_hi = gates.astype(bf16)
    g_lo = (gates - g_hi.astype(f32)).astype(bf16)
    ids = lax.broadcasted_iota(jnp.int32, (count, experts), 1)
    routes = routes_ref[...]
    named = ((routes[:, 0:1] == ids) | (routes[:, 1:2] == ids)).astype(f32).astype(bf16)
    rows = lax.broadcasted_iota(jnp.int32, (count, count), 0)
    cols = lax.broadcasted_iota(jnp.int32, (count, count), 1)
    rank = dot((cols < rows).astype(f32).astype(bf16), named).astype(bf16)
    spread = (
        lax.broadcasted_iota(jnp.int32, (experts, slots), 1) // CAP
        == lax.broadcasted_iota(jnp.int32, (experts, slots), 0)
    ).astype(f32).astype(bf16)
    slot = (lax.broadcasted_iota(jnp.int32, (count, slots), 1) % CAP).astype(f32)
    here = (dot(named, spread) > 0.5) & (dot(rank, spread) == slot)
    hi_ref[...] = jnp.where(here, dot(g_hi, spread), 0.0).astype(bf16)
    lo_ref[...] = jnp.where(here, dot(g_lo, spread), 0.0).astype(bf16)
    ids_t = lax.broadcasted_iota(jnp.int32, (experts, count), 0)
    routes_t = routes_t_ref[...]
    named_t = ((routes_t[0:1, :] == ids_t) | (routes_t[1:2, :] == ids_t)).astype(f32).astype(bf16)
    rank_t = dot(named_t, (rows < cols).astype(f32).astype(bf16)).astype(bf16)
    spread_t = (
        lax.broadcasted_iota(jnp.int32, (slots, experts), 0) // CAP
        == lax.broadcasted_iota(jnp.int32, (slots, experts), 1)
    ).astype(f32).astype(bf16)
    slot_t = (lax.broadcasted_iota(jnp.int32, (slots, count), 0) % CAP).astype(f32)
    here_t = (dot(spread_t, named_t) > 0.5) & (dot(spread_t, rank_t) == slot_t)
    send_ref[...] = dot(here_t.astype(f32).astype(bf16), normed).astype(bf16)


def remote(src, dst, send_sem, recv_sem, **where):
    return pltpu.make_async_remote_copy(
        src_ref=src,
        dst_ref=dst,
        send_sem=send_sem,
        recv_sem=recv_sem,
        device_id=where,
        device_id_type=pl.DeviceIdType.MESH,
    )


class Place:
    def __init__(self, zs=8, xs=4):
        self.zs, self.xs = zs, xs
        self.me = lax.axis_index("ctx")
        self.y = lax.axis_index("ch")
        self.core = self.me % 2
        self.chip = self.me // 2
        self.z = self.chip // xs
        self.x = self.chip % xs
        self.twin = self.me + 1 - 2 * self.core

    def at(self, dz, dx):
        return (self.z + dz + self.zs) % self.zs * self.xs + (self.x + dx + self.xs) % self.xs


def greet(place, zs, xs, ys):
    barrier = pltpu.get_barrier_semaphore()

    def tell(**where):
        pl.semaphore_signal(barrier, inc=1, device_id=where, device_id_type=pl.DeviceIdType.MESH)

    def chip(i, carry):
        tell(ctx=place.at(i // xs, i % xs) * 2 + place.core)
        return carry

    lax.fori_loop(1, zs * xs, chip, 0)
    tell(ctx=place.twin)
    for dy in range(1, ys):
        tell(ch=(place.y + dy) % ys)
    pl.semaphore_wait(barrier, zs * xs - 1 + 1 + ys - 1)


def offsets(q, half, j):
    if half == 0:
        return 4 - q, j
    return (4 + q if q else 0), (j + 1) % 4


def each(q, act):
    for half in range(2):

        def one(j, carry):
            dz, dx = offsets(q, half, j)
            act(q * 8 + half * 4 + j, dz, dx)
            return carry

        lax.fori_loop(0, 3 if q == 0 and half == 1 else 4, one, 0)


def experts_kernel(
    send, hi, lo, up_ref, down_ref, out, got, twin_got, part, twin_part, summed, back, moe, landed, own,
    send_sem, got_sem, fs_sem, fr_sem, ps_sem, pr_sem, rs_sem, back_sem, ms_sem, mr_sem, local_sem,
):
    place = Place()
    me, core, chip, y = place.me, place.core, place.chip, place.y
    chunk = 8
    rows = chunk * CAP
    greet(place, 8, 4, 4)
    for q in range(4):

        def dispatch(slot, dz, dx):
            to = place.at(dz, dx)
            remote(send.at[to], got.at[slot], send_sem, got_sem.at[q], ctx=to * 2 + core).start()

        each(q, dispatch)
    keep = pltpu.make_async_copy(send.at[chip], got.at[7], local_sem.at[0])
    keep.start()
    keep_back = pltpu.make_async_copy(summed.at[7], back.at[chip], local_sem.at[1])

    def mlp(block):
        x = block.reshape(rows, block.shape[-1])
        hidden = jax.nn.gelu(dot(x, up_ref[...]), approximate=True).astype(bf16)
        return dot(hidden, down_ref[...])

    for q in range(4):
        slots = pl.ds(q * chunk, chunk)
        here = pl.ds(q * chunk, 7) if q == 0 else slots
        remote(send.at[here], got.at[here], send_sem, got_sem.at[q], ctx=me).wait_recv()
        if q == 0:
            keep.wait()
        share = remote(got.at[slots], twin_got.at[slots], fs_sem.at[q], fr_sem.at[q], ctx=place.twin)
        share.start()
        own[...] = mlp(got[slots])
        share.wait_recv()
        part[slots] = mlp(twin_got[slots]).astype(bf16).reshape(chunk, CAP, -1)
        give = remote(part.at[slots], twin_part.at[slots], ps_sem.at[q], pr_sem.at[q], ctx=place.twin)
        give.start()
        give.wait_recv()
        total = own[...].reshape(chunk, CAP, -1) + twin_part[slots].astype(f32)
        summed[slots] = total.astype(bf16)

        def give_back(slot, dz, dx):
            to = place.at(-dz, -dx)
            remote(summed.at[slot], back.at[chip], rs_sem, back_sem, ctx=to * 2 + core).start()

        each(q, give_back)
        if q == 0:
            keep_back.start()
        share.wait_send()
        give.wait_send()
    keep_back.wait()
    others = pl.ds(0, 31)
    remote(summed.at[others], back.at[others], rs_sem, back_sem, ctx=me).wait_recv()
    gathered = back[...].reshape(32 * CAP, -1)
    result = (dot(hi[...], gathered) + dot(lo[...], gathered)).astype(bf16)
    width = moe.shape[-1]
    for k in range(4):
        moe[k] = result[:, k * width : (k + 1) * width]
    copies = []
    for dy in range(1, 4):
        to = (y + dy) % 4
        copies.append(remote(moe.at[to], landed.at[y], ms_sem.at[dy - 1], mr_sem.at[dy - 1], ch=to))
        copies[-1].start()
    landed[y] = moe[y]
    for copy in copies:
        copy.wait()
    out[...] = landed[...].reshape(out.shape)
    remote(send.at[others], got.at[others], send_sem, got_sem.at[0], ctx=me).wait_send()
    remote(summed.at[others], back.at[others], rs_sem, back_sem, ctx=me).wait_send()


def call(kernel, out_shape, *args, scratch=()):
    return pl.pallas_call(
        kernel,
        out_shape=out_shape,
        in_specs=[pl.BlockSpec(memory_space=pltpu.VMEM)] * len(args),
        out_specs=jax.tree.map(lambda _: pl.BlockSpec(memory_space=pltpu.VMEM), out_shape),
        scratch_shapes=list(scratch),
    )(*args)


def body(signal, gate_v, taps, skip, norm_gain, router, w_up, w_down, routes):
    tok_dev, ch_dev = signal.shape
    shards = lax.axis_size("ctx")
    chans = ch_dev // shards
    experts = router.shape[1]
    width = norm_gain.shape[0]
    shape = jax.ShapeDtypeStruct
    constants = dft_constants(shards, tok_dev, chans)

    sig_t = signal.T.reshape(shards, chans, tok_dev)
    tap_t = taps.astype(bf16).T.reshape(shards, chans, tok_dev)
    packed = jnp.concatenate([sig_t, tap_t], axis=1)
    fields = lax.all_to_all(packed, "ctx", split_axis=0, concat_axis=0, tiled=True)
    conv = call(
        lambda *refs: conv_kernel(shards, chans, *refs),
        shape((shards * chans, tok_dev), bf16),
        fields.reshape(shards * 2 * chans, tok_dev),
        *constants,
        scratch=[pltpu.VMEM((2 * chans * shards, tok_dev), bf16)] * 2,
    )
    conv = lax.all_to_all(
        conv.reshape(shards, chans, tok_dev), "ctx", split_axis=0, concat_axis=0, tiled=True
    )
    conv = conv.reshape(ch_dev, tok_dev).T.astype(f32)
    mixed = (gate_v.astype(f32) * (conv + skip * signal.astype(f32))).astype(bf16)
    full_rows = lax.all_to_all(mixed, "ch", split_axis=0, concat_axis=1, tiled=True)
    slots = experts * CAP
    rows = full_rows.shape[0]
    send, hi, lo = call(
        lambda *refs: route_kernel(experts, *refs),
        (shape((slots, width), bf16), shape((rows, slots), bf16), shape((rows, slots), bf16)),
        full_rows,
        norm_gain[None, :],
        router,
        routes,
        routes.T,
    )
    blocks = (experts, CAP, width)
    dma = pltpu.SemaphoreType.DMA
    moe_out = pl.pallas_call(
        experts_kernel,
        out_shape=shape((tok_dev, ch_dev), bf16),
        in_specs=[pl.BlockSpec(memory_space=pltpu.VMEM)] * 5,
        out_specs=pl.BlockSpec(memory_space=pltpu.VMEM),
        scratch_shapes=[pltpu.VMEM(blocks, bf16)] * 6
        + [pltpu.VMEM((4, rows, ch_dev), bf16)] * 2
        + [
            pltpu.VMEM((rows, width), f32),
            dma,
            dma((4,)),
            dma((4,)),
            dma((4,)),
            dma((4,)),
            dma((4,)),
            dma,
            dma,
            dma((3,)),
            dma((3,)),
            dma((2,)),
        ],
        compiler_params=pltpu.CompilerParams(collective_id=0, has_side_effects=True),
    )(send.reshape(blocks), hi, lo, w_up[0], w_down[0])
    return (mixed, moe_out)


def solution(mesh):
    in_specs = (
        P("ctx", "ch"),
        P("ctx", "ch"),
        P("ctx", "ch"),
        P("ch"),
        P(),
        P(),
        P("ctx", None, None),
        P("ctx", None, None),
        P(("ctx", "ch"), None),
    )
    out_specs = (P("ctx", "ch"), P("ctx", "ch"))
    return jax.shard_map(body, mesh=mesh, in_specs=in_specs, out_specs=out_specs, check_vma=False)
```

```python
import math

import jax
import jax.numpy as jnp
import numpy as np
from jax import lax
from jax.experimental import pallas as pl
from jax.experimental.pallas import tpu as pltpu
from jax.sharding import PartitionSpec as P

CAP = 16
bf16 = jnp.bfloat16
f32 = jnp.float32


def dft_constants(shards, tok, chans):
    total = shards * tok
    fields = 2 * chans
    row = np.arange(shards)
    col = np.arange(tok)
    outer = 2.0 * np.pi * row[None, :] * (row[:, None] + 0.25) / shards
    first = np.concatenate([np.cos(outer), -np.sin(outer)], axis=0)
    first = np.repeat(first, fields, axis=1)
    last = np.concatenate([np.cos(outer.T), -np.sin(outer.T)], axis=1) / total
    last = np.repeat(last, fields, axis=0)
    turn = 2.0 * np.pi * (row[:, None] + 0.25) * col[None, :] / total
    inner = 2.0 * np.pi * ((col[:, None] * col[None, :]) % tok) / tok
    as16 = lambda a: jnp.asarray(a.astype(np.float32), bf16)
    as32 = lambda a: jnp.asarray(a.astype(np.float32))
    return (
        as16(first),
        as32(np.cos(turn)),
        as32(-np.sin(turn)),
        as16(np.cos(inner)),
        as16(np.sin(inner)),
        as16(last),
    )


def dot(a, b):
    return jnp.dot(a, b, preferred_element_type=f32)


def iota(shape, axis):
    return lax.broadcasted_iota(jnp.int32, shape, axis)


def one_hot(mask):
    return mask.astype(f32).astype(bf16)


def contract(a, b, axis_a, axis_b):
    return lax.dot_general(a, b, (((axis_a,), (axis_b,)), ((), ())), preferred_element_type=f32)


def pack(signal, taps, shards, fields):
    chans = fields // 2
    shape = (shards * fields, signal.shape[1])
    row, chan = iota(shape, 0), iota(shape, 1)
    field = row % fields
    mine = row // fields * chans + field % chans == chan
    sig = contract(one_hot(mine & (field < chans)), signal, 1, 1)
    tap = contract(one_hot(mine & (field >= chans)), taps.astype(bf16), 1, 1)
    return sig + tap


def convolve(data, tables, re_ref, im_ref, shards, chans):
    first, tr, ti, cos, sin, last = (table[...] for table in tables)
    fields = 2 * chans
    tok = data.shape[1]
    lane = iota(first.shape, 1) % fields
    for field in range(fields):
        g = dot(jnp.where(lane == field, first, jnp.zeros_like(first)), data)
        g_re, g_im = g[:shards], g[shards:]
        rows = pl.ds(field * shards, shards)
        re_ref[rows, :] = (g_re * tr - g_im * ti).astype(bf16)
        im_ref[rows, :] = (g_re * ti + g_im * tr).astype(bf16)
    re, im = re_ref[...], im_ref[...]
    x_re = dot(re, cos) + dot(im, sin)
    x_im = dot(im, cos) - dot(re, sin)
    half = chans * shards
    p_re = (x_re[:half] * x_re[half:] - x_im[:half] * x_im[half:]).astype(bf16)
    p_im = (x_re[:half] * x_im[half:] + x_im[:half] * x_re[half:]).astype(bf16)
    g_re = dot(p_re, cos) - dot(p_im, sin)
    g_im = dot(p_im, cos) + dot(p_re, sin)
    row = iota(last.shape, 0) % fields
    total = jnp.zeros((shards * fields, tok // 2), f32)
    for chan in range(chans):
        rows = slice(chan * shards, (chan + 1) * shards)
        a = (g_re[rows] * tr + g_im[rows] * ti).astype(bf16)
        b = (g_im[rows] * tr - g_re[rows] * ti).astype(bf16)
        both = jnp.concatenate([a, b], axis=0)
        for side in range(2):
            table = jnp.where(row == side * chans + chan, last, jnp.zeros_like(last))
            total += dot(table, both[:, side * (tok // 2) : (side + 1) * (tok // 2)])
    return total


def unpack(data, side, fields):
    chans = fields // 2
    shape = (data.shape[0], data.shape[0] // fields * chans)
    row, chan = iota(shape, 0), iota(shape, 1)
    field = row % fields
    mine = (row // fields * chans + field % chans == chan) & (field // chans == side)
    return contract(data, one_hot(mine), 0, 0)


def route(x, gain, router, routes, routes_t):
    count = x.shape[0]
    experts = router.shape[1]
    slots = experts * CAP
    scale = lax.rsqrt(jnp.mean(x * x, axis=-1, keepdims=True) + 1e-05)
    normed = (x * scale * gain).astype(bf16)
    logits = jnp.dot(
        normed.astype(f32), router, precision=lax.Precision.HIGHEST, preferred_element_type=f32
    )
    gates = jax.nn.sigmoid(logits)
    g_hi = gates.astype(bf16)
    g_lo = (gates - g_hi.astype(f32)).astype(bf16)
    ids = iota((count, experts), 1)
    named = one_hot((routes[:, 0:1] == ids) | (routes[:, 1:2] == ids))
    rows, cols = iota((count, count), 0), iota((count, count), 1)
    rank = dot(one_hot(cols < rows), named).astype(bf16)
    spread = one_hot(iota((experts, slots), 1) // CAP == iota((experts, slots), 0))
    slot = (iota((count, slots), 1) % CAP).astype(f32)
    here = (dot(named, spread) > 0.5) & (dot(rank, spread) == slot)
    hi = jnp.where(here, dot(g_hi, spread), 0.0).astype(bf16)
    lo = jnp.where(here, dot(g_lo, spread), 0.0).astype(bf16)
    ids_t = iota((experts, count), 0)
    named_t = one_hot((routes_t[0:1, :] == ids_t) | (routes_t[1:2, :] == ids_t))
    rank_t = dot(named_t, one_hot(rows < cols)).astype(bf16)
    spread_t = one_hot(iota((slots, experts), 0) // CAP == iota((slots, experts), 1))
    slot_t = (iota((slots, count), 0) % CAP).astype(f32)
    here_t = (dot(spread_t, named_t) > 0.5) & (dot(spread_t, rank_t) == slot_t)
    return dot(one_hot(here_t), normed).astype(bf16), hi, lo


def remote(src, dst, send_sem, recv_sem, **where):
    return pltpu.make_async_remote_copy(
        src_ref=src,
        dst_ref=dst,
        send_sem=send_sem,
        recv_sem=recv_sem,
        device_id=where,
        device_id_type=pl.DeviceIdType.MESH,
    )


class Place:
    def __init__(self, zs=8, xs=4):
        self.zs, self.xs = zs, xs
        self.me = lax.axis_index("ctx")
        self.y = lax.axis_index("ch")
        self.core = self.me % 2
        self.chip = self.me // 2
        self.z = self.chip // xs
        self.x = self.chip % xs
        self.twin = self.me + 1 - 2 * self.core

    def at(self, dz, dx):
        return (self.z + dz + self.zs) % self.zs * self.xs + (self.x + dx + self.xs) % self.xs


def greet(place, count, ys):
    barrier = pltpu.get_barrier_semaphore()

    def tell(**where):
        pl.semaphore_signal(barrier, inc=1, device_id=where, device_id_type=pl.DeviceIdType.MESH)

    def shard(i, carry):
        tell(ctx=(place.me + i) % count)
        return carry

    lax.fori_loop(1, count, shard, 0)
    for dy in range(1, ys):
        tell(ch=(place.y + dy) % ys)
    return lambda: pl.semaphore_wait(barrier, count - 1 + ys - 1)


def offsets(q, half, j):
    if half == 0:
        return 4 - q, j
    return (4 + q if q else 0), (j + 1) % 4


def each(q, act):
    for half in range(2):

        def one(j, carry):
            dz, dx = offsets(q, half, j)
            act(q * 8 + half * 4 + j, dz, dx)
            return carry

        lax.fori_loop(0, 3 if q == 0 and half == 1 else 4, one, 0)


def split(refs, far, outs, conv, moe, sems):
    refs = list(refs)
    cut = [refs[:far], refs[far : far + outs]]
    rest = refs[far + outs :]
    first = rest[:conv]
    cut.append((first[: far + 1], *first[far + 1 :]))
    cut.append(rest[conv : conv + moe])
    cut.append(rest[conv + moe :])
    return cut


def layer_kernel(
    signal, taps, skip, gain, router, routes, routes_t, gate_hbm, *rest
):
    place = Place()
    me, core, chip, y = place.me, place.core, place.chip, place.y
    (
        far, (mixed_out, out),
        (near, packed, fields, re_ref, im_ref, conv_out, conv_in, mixed, full),
        (send, hi, lo, got, twin_got, part, twin_part, summed, back, moe, landed, own),
        (far_sem, local_sem, conv_sem, xs_sem, xr_sem, send_sem, got_sem, fs_sem, fr_sem, ps_sem, pr_sem,
         rs_sem, back_sem, ms_sem, mr_sem),
    ) = split(rest, 8, 2, 17, 12, 15)
    shards, width_ch = 64, signal.shape[1]
    chans = width_ch // shards
    ready = greet(place, shards, 4)
    fetches = [
        pltpu.make_async_copy(a, b, far_sem.at[i]) for i, (a, b) in enumerate(zip((gate_hbm, *far), near))
    ]
    for fetch in fetches:
        fetch.start()
    gate, tables, up_ref, down_ref = near[0], near[1:7], near[7], near[8]
    packed[...] = pack(signal[...], taps[...], shards, 2 * chans).reshape(packed.shape).astype(bf16)
    ready()

    def spread_out(source, target, ss, rs):
        def both(to):
            for side in range(2):
                where = to * 2 + side
                remote(source.at[where], target.at[me], ss, rs, ctx=where).start()

        for q in range(4):
            each(q, lambda slot, dz, dx: both(place.at(dz, dx)))
        remote(source.at[place.twin], target.at[me], ss, rs, ctx=place.twin).start()
        stay = pltpu.make_async_copy(source.at[me], target.at[me], local_sem.at[2])
        stay.start()
        most = pl.ds(0, shards - 1)
        whole = remote(source.at[most], target.at[most], ss, rs, ctx=place.twin)
        whole.wait_recv()
        stay.wait()
        return whole

    whole = spread_out(packed, fields, conv_sem.at[0], conv_sem.at[1])
    for fetch in fetches:
        fetch.wait()
    data = fields[...].astype(f32).reshape(shards * 2 * chans, -1).astype(bf16)
    total = convolve(data, tables, re_ref, im_ref, shards, chans)
    conv_out[...] = total.reshape(conv_out.shape).astype(bf16)
    whole_back = spread_out(conv_out, conv_in, conv_sem.at[2], conv_sem.at[3])
    whole.wait_send()
    data = conv_in[...].astype(f32).reshape(shards * 2 * chans, -1).astype(bf16)
    for side in range(2):
        conv = unpack(data, side, 2 * chans)
        count = conv.shape[0]
        span = slice(side * count, (side + 1) * count)
        sig = signal[span, :].astype(f32)
        value = (gate[span, :].astype(f32) * (conv + skip[...] * sig)).astype(bf16)
        mixed_out[span, :] = value
        mixed[2 * side] = value[: count // 2]
        mixed[2 * side + 1] = value[count // 2 :]
    copies = []
    for dy in range(1, 4):
        to = (y + dy) % 4
        copies.append(remote(mixed.at[to], full.at[y], xs_sem.at[dy - 1], xr_sem.at[dy - 1], ch=to))
        copies[-1].start()
    full[y] = mixed[y]
    for copy in copies:
        copy.wait()
    whole_back.wait_send()
    x = jnp.concatenate([full[k] for k in range(4)], axis=1).astype(f32)
    rows_out, hi[...], lo[...] = route(x, gain[...], router[...], routes[...], routes_t[...])
    send[...] = rows_out.reshape(send.shape)
    chunk = 8
    rows = chunk * CAP
    for q in range(4):

        def dispatch(slot, dz, dx):
            to = place.at(dz, dx)
            remote(send.at[to], got.at[slot], send_sem, got_sem.at[q], ctx=to * 2 + core).start()

        each(q, dispatch)
    keep = pltpu.make_async_copy(send.at[chip], got.at[7], local_sem.at[0])
    keep.start()
    keep_back = pltpu.make_async_copy(summed.at[7], back.at[chip], local_sem.at[1])

    def mlp(block):
        x = block.reshape(rows, block.shape[-1])
        hidden = jax.nn.gelu(dot(x, up_ref[...]), approximate=True).astype(bf16)
        return dot(hidden, down_ref[...])

    for q in range(4):
        slots = pl.ds(q * chunk, chunk)
        here = pl.ds(q * chunk, 7) if q == 0 else slots
        remote(send.at[here], got.at[here], send_sem, got_sem.at[q], ctx=me).wait_recv()
        if q == 0:
            keep.wait()
        share = remote(got.at[slots], twin_got.at[slots], fs_sem.at[q], fr_sem.at[q], ctx=place.twin)
        share.start()
        own[...] = mlp(got[slots])
        share.wait_recv()
        part[slots] = mlp(twin_got[slots]).astype(bf16).reshape(chunk, CAP, -1)
        give = remote(part.at[slots], twin_part.at[slots], ps_sem.at[q], pr_sem.at[q], ctx=place.twin)
        give.start()
        give.wait_recv()
        total = own[...].reshape(chunk, CAP, -1) + twin_part[slots].astype(f32)
        summed[slots] = total.astype(bf16)

        def give_back(slot, dz, dx):
            to = place.at(-dz, -dx)
            remote(summed.at[slot], back.at[chip], rs_sem, back_sem, ctx=to * 2 + core).start()

        each(q, give_back)
        if q == 0:
            keep_back.start()
        share.wait_send()
        give.wait_send()
    keep_back.wait()
    others = pl.ds(0, 31)
    remote(summed.at[others], back.at[others], rs_sem, back_sem, ctx=me).wait_recv()
    gathered = back[...].reshape(32 * CAP, -1)
    result = (dot(hi[...], gathered) + dot(lo[...], gathered)).astype(bf16)
    width = moe.shape[-1]
    for k in range(4):
        moe[k] = result[:, k * width : (k + 1) * width]
    copies = []
    for dy in range(1, 4):
        to = (y + dy) % 4
        copies.append(remote(moe.at[to], landed.at[y], ms_sem.at[dy - 1], mr_sem.at[dy - 1], ch=to))
        copies[-1].start()
    landed[y] = moe[y]
    for copy in copies:
        copy.wait()
    out[...] = landed[...].reshape(out.shape)
    remote(send.at[others], got.at[others], send_sem, got_sem.at[0], ctx=me).wait_send()
    remote(summed.at[others], back.at[others], rs_sem, back_sem, ctx=me).wait_send()


def call(kernel, out_shape, *args, scratch=()):
    return pl.pallas_call(
        kernel,
        out_shape=out_shape,
        in_specs=[pl.BlockSpec(memory_space=pltpu.VMEM)] * len(args),
        out_specs=jax.tree.map(lambda _: pl.BlockSpec(memory_space=pltpu.VMEM), out_shape),
        scratch_shapes=list(scratch),
    )(*args)


def body(signal, gate_v, taps, skip, norm_gain, router, w_up, w_down, routes):
    tok_dev, ch_dev = signal.shape
    shards = lax.axis_size("ctx")
    groups = lax.axis_size("ch")
    chans = ch_dev // shards
    experts = router.shape[1]
    width = norm_gain.shape[0]
    rows = tok_dev // groups
    shape = jax.ShapeDtypeStruct
    far = (*dft_constants(shards, tok_dev, chans), w_up[0], w_down[0])
    blocks = (experts, CAP, width)
    dma = pltpu.SemaphoreType.DMA
    vmem = pltpu.VMEM
    here = pl.BlockSpec(memory_space=vmem)
    there = pl.BlockSpec(memory_space=pl.ANY)
    local = shape((tok_dev, ch_dev), bf16)
    mixed, moe_out = pl.pallas_call(
        layer_kernel,
        out_shape=(local, local),
        in_specs=[here] * 7 + [there] * (1 + len(far)),
        out_specs=(here, here),
        scratch_shapes=[vmem(gate_v.shape, gate_v.dtype)]
        + [vmem(a.shape, a.dtype) for a in far]
        + [vmem((shards, 2 * chans, tok_dev), bf16)] * 2
        + [vmem((2 * chans * shards, tok_dev), bf16)] * 2
        + [vmem((shards, 2 * chans, tok_dev // 2), bf16)] * 2
        + [vmem((groups, rows, ch_dev), bf16)] * 2
        + [vmem(blocks, bf16)]
        + [vmem((rows, experts * CAP), bf16)] * 2
        + [vmem(blocks, bf16)] * 6
        + [vmem((groups, rows, ch_dev), bf16)] * 2
        + [vmem((rows, width), f32)]
        + [dma((9,)), dma((3,)), dma((4,)), dma((3,)), dma((3,)), dma]
        + [dma((4,))] * 5
        + [dma, dma, dma((3,)), dma((3,))],
        compiler_params=pltpu.CompilerParams(collective_id=0, has_side_effects=True),
    )(signal, taps, skip[None, :], norm_gain[None, :], router, routes, routes.T, gate_v, *far)
    return (mixed, moe_out)


def solution(mesh):
    in_specs = (
        P("ctx", "ch"),
        P("ctx", "ch"),
        P("ctx", "ch"),
        P("ch"),
        P(),
        P(),
        P("ctx", None, None),
        P("ctx", None, None),
        P(("ctx", "ch"), None),
    )
    out_specs = (P("ctx", "ch"), P("ctx", "ch"))
    return jax.shard_map(body, mesh=mesh, in_specs=in_specs, out_specs=out_specs, check_vma=False)
```

```python
import math

import jax
import jax.numpy as jnp
import numpy as np
from jax import lax
from jax.experimental import pallas as pl
from jax.experimental.pallas import tpu as pltpu
from jax.sharding import PartitionSpec as P

CAP = 16
bf16 = jnp.bfloat16
f32 = jnp.float32


def dft_constants(shards, tok, chans):
    total = shards * tok
    fields = 2 * chans
    row = np.arange(shards)
    col = np.arange(tok)
    outer = 2.0 * np.pi * row[None, :] * (row[:, None] + 0.25) / shards
    first = np.concatenate([np.cos(outer), -np.sin(outer)], axis=0)
    first = np.repeat(first, fields, axis=1)
    last = np.concatenate([np.cos(outer.T), -np.sin(outer.T)], axis=1) / total
    last = np.repeat(last, fields, axis=0)
    turn = 2.0 * np.pi * (row[:, None] + 0.25) * col[None, :] / total
    inner = 2.0 * np.pi * ((col[:, None] * col[None, :]) % tok) / tok
    as16 = lambda a: jnp.asarray(a.astype(np.float32), bf16)
    as32 = lambda a: jnp.asarray(a.astype(np.float32))
    return (
        as16(first),
        as32(np.cos(turn)),
        as32(-np.sin(turn)),
        as16(np.cos(inner)),
        as16(np.sin(inner)),
        as16(last),
    )


def dot(a, b):
    return jnp.dot(a, b, preferred_element_type=f32)


def iota(shape, axis):
    return lax.broadcasted_iota(jnp.int32, shape, axis)


def one_hot(mask):
    return mask.astype(f32).astype(bf16)


def contract(a, b, axis_a, axis_b):
    return lax.dot_general(a, b, (((axis_a,), (axis_b,)), ((), ())), preferred_element_type=f32)


def pack(signal, taps, shards, fields):
    chans = fields // 2
    shape = (shards * fields, signal.shape[1])
    row, chan = iota(shape, 0), iota(shape, 1)
    field = row % fields
    mine = row // fields * chans + field % chans == chan
    sig = contract(one_hot(mine & (field < chans)), signal, 1, 1)
    tap = contract(one_hot(mine & (field >= chans)), taps.astype(bf16), 1, 1)
    return sig + tap


def convolve(data, tables, re_ref, im_ref, shards, chans):
    first, tr, ti, cos, sin, last = (table[...] for table in tables)
    fields = 2 * chans
    tok = data.shape[1]
    lane = iota(first.shape, 1) % fields
    for field in range(fields):
        g = dot(jnp.where(lane == field, first, jnp.zeros_like(first)), data)
        g_re, g_im = g[:shards], g[shards:]
        rows = pl.ds(field * shards, shards)
        re_ref[rows, :] = (g_re * tr - g_im * ti).astype(bf16)
        im_ref[rows, :] = (g_re * ti + g_im * tr).astype(bf16)
    re, im = re_ref[...], im_ref[...]
    x_re = dot(re, cos) + dot(im, sin)
    x_im = dot(im, cos) - dot(re, sin)
    half = chans * shards
    p_re = (x_re[:half] * x_re[half:] - x_im[:half] * x_im[half:]).astype(bf16)
    p_im = (x_re[:half] * x_im[half:] + x_im[:half] * x_re[half:]).astype(bf16)
    g_re = dot(p_re, cos) - dot(p_im, sin)
    g_im = dot(p_im, cos) + dot(p_re, sin)
    row = iota(last.shape, 0) % fields
    total = jnp.zeros((shards * fields, tok // 2), f32)
    for chan in range(chans):
        rows = slice(chan * shards, (chan + 1) * shards)
        a = (g_re[rows] * tr + g_im[rows] * ti).astype(bf16)
        b = (g_im[rows] * tr - g_re[rows] * ti).astype(bf16)
        both = jnp.concatenate([a, b], axis=0)
        for side in range(2):
            table = jnp.where(row == side * chans + chan, last, jnp.zeros_like(last))
            total += dot(table, both[:, side * (tok // 2) : (side + 1) * (tok // 2)])
    return total


def unpack(data, side, fields):
    chans = fields // 2
    shape = (data.shape[0], data.shape[0] // fields * chans)
    row, chan = iota(shape, 0), iota(shape, 1)
    field = row % fields
    mine = (row // fields * chans + field % chans == chan) & (field // chans == side)
    return contract(data, one_hot(mine), 0, 0)


def slots_of(routes_t, experts):
    count = routes_t.shape[1]
    slots = experts * CAP
    ids = iota((experts, count), 0)
    named = one_hot((routes_t[0:1, :] == ids) | (routes_t[1:2, :] == ids))
    rank = dot(named, one_hot(iota((count, count), 0) < iota((count, count), 1))).astype(bf16)
    spread = one_hot(iota((slots, experts), 0) // CAP == iota((slots, experts), 1))
    slot = (iota((slots, count), 0) % CAP).astype(f32)
    return one_hot((dot(spread, named) > 0.5) & (dot(spread, rank) == slot))


def normalize(x, gain):
    scale = lax.rsqrt(jnp.mean(x * x, axis=-1, keepdims=True) + 1e-05)
    return (x * scale * gain).astype(bf16)


def gates_of(normed, router_t, here):
    count = normed.shape[0]
    experts = router_t.shape[0]
    slots = experts * CAP
    logits = lax.dot_general(
        router_t,
        normed.astype(f32),
        (((1,), (1,)), ((), ())),
        precision=lax.Precision.HIGHEST,
        preferred_element_type=f32,
    )
    gates = jax.nn.sigmoid(logits)
    high = gates.astype(bf16)
    low = (gates - high.astype(f32)).astype(bf16)
    spread = one_hot(iota((slots, experts), 0) // CAP == iota((slots, experts), 1))
    turn = one_hot(iota((count, count), 0) == iota((count, count), 1))
    chosen = here > 0.5
    parts = (jnp.where(chosen, dot(spread, part), 0.0).astype(bf16) for part in (high, low))
    return tuple(contract(turn, part, 1, 1).astype(bf16) for part in parts)


def remote(src, dst, send_sem, recv_sem, **where):
    return pltpu.make_async_remote_copy(
        src_ref=src,
        dst_ref=dst,
        send_sem=send_sem,
        recv_sem=recv_sem,
        device_id=where,
        device_id_type=pl.DeviceIdType.MESH,
    )


class Place:
    def __init__(self, zs=8, xs=4):
        self.zs, self.xs = zs, xs
        self.me = lax.axis_index("ctx")
        self.y = lax.axis_index("ch")
        self.core = self.me % 2
        self.chip = self.me // 2
        self.z = self.chip // xs
        self.x = self.chip % xs
        self.twin = self.me + 1 - 2 * self.core

    def at(self, dz, dx):
        return (self.z + dz + self.zs) % self.zs * self.xs + (self.x + dx + self.xs) % self.xs


def greet(place, count, ys):
    barrier = pltpu.get_barrier_semaphore()

    def tell(**where):
        pl.semaphore_signal(barrier, inc=1, device_id=where, device_id_type=pl.DeviceIdType.MESH)

    def shard(i, carry):
        tell(ctx=(place.me + i) % count)
        return carry

    lax.fori_loop(1, count, shard, 0)
    for dy in range(1, ys):
        tell(ch=(place.y + dy) % ys)
    return lambda: pl.semaphore_wait(barrier, count - 1 + ys - 1)


def offsets(q, half, j):
    if half == 0:
        return 4 - q, j
    return (4 + q if q else 0), (j + 1) % 4


def each(q, act):
    for half in range(2):

        def one(j, carry):
            dz, dx = offsets(q, half, j)
            act(q * 8 + half * 4 + j, dz, dx)
            return carry

        lax.fori_loop(0, 3 if q == 0 and half == 1 else 4, one, 0)


def split(refs, far, outs, conv, moe, sems):
    refs = list(refs)
    cut = [refs[:far], refs[far : far + outs]]
    rest = refs[far + outs :]
    first = rest[:conv]
    cut.append((first[: far + 1], *first[far + 1 :]))
    cut.append(rest[conv : conv + moe])
    cut.append(rest[conv + moe :])
    return cut


def layer_kernel(
    signal, taps, skip, gain, router_t, routes_t, gate_hbm, *rest
):
    place = Place()
    me, core, chip, y = place.me, place.core, place.chip, place.y
    (
        far, (mixed_out, out),
        (near, packed, fields, re_ref, im_ref, conv_out, conv_in, mixed, full),
        (send, here, got, twin_got, part, twin_part, summed, back, moe, landed, own),
        (far_sem, local_sem, conv_sem, xs_sem, xr_sem, send_sem, got_sem, fs_sem, fr_sem, ps_sem, pr_sem,
         rs_sem, back_sem, ms_sem, mr_sem),
    ) = split(rest, 8, 2, 17, 11, 15)
    shards, width_ch = 64, signal.shape[1]
    chans = width_ch // shards
    ready = greet(place, shards, 4)
    fetches = [
        pltpu.make_async_copy(a, b, far_sem.at[i]) for i, (a, b) in enumerate(zip((gate_hbm, *far), near))
    ]
    for fetch in fetches:
        fetch.start()
    gate, tables, up_ref, down_ref = near[0], near[1:7], near[7], near[8]
    packed[...] = pack(signal[...], taps[...], shards, 2 * chans).reshape(packed.shape).astype(bf16)
    here[...] = slots_of(routes_t[...], router_t.shape[0])
    ready()

    def spread_out(source, target, ss, rs):
        def both(to):
            for side in range(2):
                where = to * 2 + side
                remote(source.at[where], target.at[me], ss, rs, ctx=where).start()

        for q in range(4):
            each(q, lambda slot, dz, dx: both(place.at(dz, dx)))
        remote(source.at[place.twin], target.at[me], ss, rs, ctx=place.twin).start()
        stay = pltpu.make_async_copy(source.at[me], target.at[me], local_sem.at[2])
        stay.start()
        most = pl.ds(0, shards - 1)
        whole = remote(source.at[most], target.at[most], ss, rs, ctx=place.twin)
        whole.wait_recv()
        stay.wait()
        return whole

    whole = spread_out(packed, fields, conv_sem.at[0], conv_sem.at[1])
    for fetch in fetches:
        fetch.wait()
    data = fields[...].astype(f32).reshape(shards * 2 * chans, -1).astype(bf16)
    total = convolve(data, tables, re_ref, im_ref, shards, chans)
    conv_out[...] = total.reshape(conv_out.shape).astype(bf16)
    whole_back = spread_out(conv_out, conv_in, conv_sem.at[2], conv_sem.at[3])
    whole.wait_send()
    data = conv_in[...].astype(f32).reshape(shards * 2 * chans, -1).astype(bf16)
    for side in range(2):
        conv = unpack(data, side, 2 * chans)
        count = conv.shape[0]
        span = slice(side * count, (side + 1) * count)
        sig = signal[span, :].astype(f32)
        value = (gate[span, :].astype(f32) * (conv + skip[...] * sig)).astype(bf16)
        mixed_out[span, :] = value
        for k in range(2 * side, 2 * side + 2):
            mixed[k] = value[(k % 2) * (count // 2) : (k % 2 + 1) * (count // 2)]

            @pl.when(y != k)
            def _():
                remote(mixed.at[k], full.at[y], xs_sem, xr_sem, ch=k).start()

    full[y] = mixed[y]
    trio = pl.ds(0, 3)
    quarters = remote(mixed.at[trio], full.at[trio], xs_sem, xr_sem, ch=(y + 1) % 4)
    quarters.wait_recv()
    normed = normalize(jnp.concatenate([full[k] for k in range(4)], axis=1).astype(f32), gain[...])
    send[...] = dot(here[...], normed).astype(bf16).reshape(send.shape)
    chunk = 8
    rows = chunk * CAP
    for q in range(4):

        def dispatch(slot, dz, dx):
            to = place.at(dz, dx)
            remote(send.at[to], got.at[slot], send_sem, got_sem.at[q], ctx=to * 2 + core).start()

        each(q, dispatch)
    keep = pltpu.make_async_copy(send.at[chip], got.at[7], local_sem.at[0])
    keep.start()
    keep_back = pltpu.make_async_copy(summed.at[7], back.at[chip], local_sem.at[1])
    hi, lo = gates_of(normed, router_t[...], here[...])
    quarters.wait_send()
    whole_back.wait_send()

    def mlp(block):
        x = block.reshape(rows, block.shape[-1])
        hidden = jax.nn.gelu(dot(x, up_ref[...]), approximate=True).astype(bf16)
        return dot(hidden, down_ref[...])

    for q in range(4):
        slots = pl.ds(q * chunk, chunk)
        came = pl.ds(q * chunk, 7) if q == 0 else slots
        remote(send.at[came], got.at[came], send_sem, got_sem.at[q], ctx=me).wait_recv()
        if q == 0:
            keep.wait()
        share = remote(got.at[slots], twin_got.at[slots], fs_sem.at[q], fr_sem.at[q], ctx=place.twin)
        share.start()
        own[...] = mlp(got[slots])
        share.wait_recv()
        part[slots] = mlp(twin_got[slots]).astype(bf16).reshape(chunk, CAP, -1)
        give = remote(part.at[slots], twin_part.at[slots], ps_sem.at[q], pr_sem.at[q], ctx=place.twin)
        give.start()
        give.wait_recv()
        total = own[...].reshape(chunk, CAP, -1) + twin_part[slots].astype(f32)
        summed[slots] = total.astype(bf16)

        def give_back(slot, dz, dx):
            to = place.at(-dz, -dx)
            remote(summed.at[slot], back.at[chip], rs_sem, back_sem, ctx=to * 2 + core).start()

        each(q, give_back)
        if q == 0:
            keep_back.start()
        share.wait_send()
        give.wait_send()
    keep_back.wait()
    others = pl.ds(0, 31)
    remote(summed.at[others], back.at[others], rs_sem, back_sem, ctx=me).wait_recv()
    gathered = back[...].reshape(32 * CAP, -1)
    result = (dot(hi, gathered) + dot(lo, gathered)).astype(bf16)
    width = moe.shape[-1]
    for k in range(4):
        moe[k] = result[:, k * width : (k + 1) * width]
    copies = []
    for dy in range(1, 4):
        to = (y + dy) % 4
        copies.append(remote(moe.at[to], landed.at[y], ms_sem.at[dy - 1], mr_sem.at[dy - 1], ch=to))
        copies[-1].start()
    landed[y] = moe[y]
    for copy in copies:
        copy.wait()
    out[...] = landed[...].reshape(out.shape)
    remote(send.at[others], got.at[others], send_sem, got_sem.at[0], ctx=me).wait_send()
    remote(summed.at[others], back.at[others], rs_sem, back_sem, ctx=me).wait_send()


def call(kernel, out_shape, *args, scratch=()):
    return pl.pallas_call(
        kernel,
        out_shape=out_shape,
        in_specs=[pl.BlockSpec(memory_space=pltpu.VMEM)] * len(args),
        out_specs=jax.tree.map(lambda _: pl.BlockSpec(memory_space=pltpu.VMEM), out_shape),
        scratch_shapes=list(scratch),
    )(*args)


def body(signal, gate_v, taps, skip, norm_gain, router, w_up, w_down, routes):
    tok_dev, ch_dev = signal.shape
    shards = lax.axis_size("ctx")
    groups = lax.axis_size("ch")
    chans = ch_dev // shards
    experts = router.shape[1]
    width = norm_gain.shape[0]
    rows = tok_dev // groups
    shape = jax.ShapeDtypeStruct
    far = (*dft_constants(shards, tok_dev, chans), w_up[0], w_down[0])
    blocks = (experts, CAP, width)
    dma = pltpu.SemaphoreType.DMA
    vmem = pltpu.VMEM
    here = pl.BlockSpec(memory_space=vmem)
    there = pl.BlockSpec(memory_space=pl.ANY)
    local = shape((tok_dev, ch_dev), bf16)
    mixed, moe_out = pl.pallas_call(
        layer_kernel,
        out_shape=(local, local),
        in_specs=[here] * 6 + [there] * (1 + len(far)),
        out_specs=(here, here),
        scratch_shapes=[vmem(gate_v.shape, gate_v.dtype)]
        + [vmem(a.shape, a.dtype) for a in far]
        + [vmem((shards, 2 * chans, tok_dev), bf16)] * 2
        + [vmem((2 * chans * shards, tok_dev), bf16)] * 2
        + [vmem((shards, 2 * chans, tok_dev // 2), bf16)] * 2
        + [vmem((groups, rows, ch_dev), bf16)] * 2
        + [vmem(blocks, bf16)]
        + [vmem((experts * CAP, rows), bf16)]
        + [vmem(blocks, bf16)] * 6
        + [vmem((groups, rows, ch_dev), bf16)] * 2
        + [vmem((rows, width), f32)]
        + [dma((9,)), dma((3,)), dma((4,)), dma, dma, dma]
        + [dma((4,))] * 5
        + [dma, dma, dma((3,)), dma((3,))],
        compiler_params=pltpu.CompilerParams(collective_id=0, has_side_effects=True),
    )(signal, taps, skip[None, :], norm_gain[None, :], router.T, routes.T, gate_v, *far)
    return (mixed, moe_out)


def solution(mesh):
    in_specs = (
        P("ctx", "ch"),
        P("ctx", "ch"),
        P("ctx", "ch"),
        P("ch"),
        P(),
        P(),
        P("ctx", None, None),
        P("ctx", None, None),
        P(("ctx", "ch"), None),
    )
    out_specs = (P("ctx", "ch"), P("ctx", "ch"))
    return jax.shard_map(body, mesh=mesh, in_specs=in_specs, out_specs=out_specs, check_vma=False)
```

```python
import math

import jax
import jax.numpy as jnp
import numpy as np
from jax import lax
from jax.experimental import pallas as pl
from jax.experimental.pallas import tpu as pltpu
from jax.sharding import PartitionSpec as P

CAP = 16
bf16 = jnp.bfloat16
f32 = jnp.float32


def dft_constants(shards, tok, chans):
    total = shards * tok
    fields = 2 * chans
    row = np.arange(shards)
    col = np.arange(tok)
    outer = 2.0 * np.pi * row[None, :] * (row[:, None] + 0.25) / shards
    first = np.concatenate([np.cos(outer), -np.sin(outer)], axis=0)
    first = np.repeat(first, fields, axis=1)
    last = np.concatenate([np.cos(outer.T), -np.sin(outer.T)], axis=1) / total
    last = np.repeat(last, fields, axis=0)
    turn = 2.0 * np.pi * (row[:, None] + 0.25) * col[None, :] / total
    inner = 2.0 * np.pi * ((col[:, None] * col[None, :]) % tok) / tok
    as16 = lambda a: jnp.asarray(a.astype(np.float32), bf16)
    as32 = lambda a: jnp.asarray(a.astype(np.float32))
    return (
        as16(first),
        as32(np.cos(turn)),
        as32(-np.sin(turn)),
        as16(np.cos(inner)),
        as16(np.sin(inner)),
        as16(last),
    )


def dot(a, b):
    return jnp.dot(a, b, preferred_element_type=f32)


def iota(shape, axis):
    return lax.broadcasted_iota(jnp.int32, shape, axis)


def one_hot(mask):
    return mask.astype(f32).astype(bf16)


def contract(a, b, axis_a, axis_b):
    return lax.dot_general(a, b, (((axis_a,), (axis_b,)), ((), ())), preferred_element_type=f32)


def pack(signal, taps, shards, fields):
    chans = fields // 2
    shape = (shards * fields, signal.shape[1])
    row, chan = iota(shape, 0), iota(shape, 1)
    field = row % fields
    mine = row // fields * chans + field % chans == chan
    sig = contract(one_hot(mine & (field < chans)), signal, 1, 1)
    tap = contract(one_hot(mine & (field >= chans)), taps.astype(bf16), 1, 1)
    return sig + tap


def convolve(data, tables, re_ref, im_ref, shards, chans):
    first, tr, ti, cos, sin, last = (table[...] for table in tables)
    fields = 2 * chans
    tok = data.shape[1]
    lane = iota(first.shape, 1) % fields
    for field in range(fields):
        g = dot(jnp.where(lane == field, first, jnp.zeros_like(first)), data)
        g_re, g_im = g[:shards], g[shards:]
        rows = pl.ds(field * shards, shards)
        re_ref[rows, :] = (g_re * tr - g_im * ti).astype(bf16)
        im_ref[rows, :] = (g_re * ti + g_im * tr).astype(bf16)
    re, im = re_ref[...], im_ref[...]
    x_re = dot(re, cos) + dot(im, sin)
    x_im = dot(im, cos) - dot(re, sin)
    half = chans * shards
    p_re = (x_re[:half] * x_re[half:] - x_im[:half] * x_im[half:]).astype(bf16)
    p_im = (x_re[:half] * x_im[half:] + x_im[:half] * x_re[half:]).astype(bf16)
    g_re = dot(p_re, cos) - dot(p_im, sin)
    g_im = dot(p_im, cos) + dot(p_re, sin)
    row = iota(last.shape, 0) % fields
    total = jnp.zeros((shards * fields, tok // 2), f32)
    for chan in range(chans):
        rows = slice(chan * shards, (chan + 1) * shards)
        a = (g_re[rows] * tr + g_im[rows] * ti).astype(bf16)
        b = (g_im[rows] * tr - g_re[rows] * ti).astype(bf16)
        both = jnp.concatenate([a, b], axis=0)
        for side in range(2):
            table = jnp.where(row == side * chans + chan, last, jnp.zeros_like(last))
            total += dot(table, both[:, side * (tok // 2) : (side + 1) * (tok // 2)])
    return total


def unpack(data, side, fields):
    chans = fields // 2
    shape = (data.shape[0], data.shape[0] // fields * chans)
    row, chan = iota(shape, 0), iota(shape, 1)
    field = row % fields
    mine = (row // fields * chans + field % chans == chan) & (field // chans == side)
    return contract(data, one_hot(mine), 0, 0)


def slots_of(routes_t, experts):
    count = routes_t.shape[1]
    slots = experts * CAP
    ids = iota((experts, count), 0)
    named = one_hot((routes_t[0:1, :] == ids) | (routes_t[1:2, :] == ids))
    rank = dot(named, one_hot(iota((count, count), 0) < iota((count, count), 1))).astype(bf16)
    spread = one_hot(iota((slots, experts), 0) // CAP == iota((slots, experts), 1))
    slot = (iota((slots, count), 0) % CAP).astype(f32)
    return one_hot((dot(spread, named) > 0.5) & (dot(spread, rank) == slot))


def normalize(x, gain):
    scale = lax.rsqrt(jnp.mean(x * x, axis=-1, keepdims=True) + 1e-05)
    return (x * scale * gain).astype(bf16)


def gates_of(normed, router_t, here):
    count = normed.shape[0]
    experts = router_t.shape[0]
    slots = experts * CAP
    logits = lax.dot_general(
        router_t,
        normed.astype(f32),
        (((1,), (1,)), ((), ())),
        precision=lax.Precision.HIGHEST,
        preferred_element_type=f32,
    )
    gates = jax.nn.sigmoid(logits)
    high = gates.astype(bf16)
    low = (gates - high.astype(f32)).astype(bf16)
    spread = one_hot(iota((slots, experts), 0) // CAP == iota((slots, experts), 1))
    turn = one_hot(iota((count, count), 0) == iota((count, count), 1))
    chosen = here > 0.5
    parts = (jnp.where(chosen, dot(spread, part), 0.0).astype(bf16) for part in (high, low))
    return tuple(contract(turn, part, 1, 1).astype(bf16) for part in parts)


def remote(src, dst, send_sem, recv_sem, **where):
    return pltpu.make_async_remote_copy(
        src_ref=src,
        dst_ref=dst,
        send_sem=send_sem,
        recv_sem=recv_sem,
        device_id=where,
        device_id_type=pl.DeviceIdType.MESH,
    )


class Place:
    def __init__(self, zs=8, xs=4):
        self.zs, self.xs = zs, xs
        self.me = lax.axis_index("ctx")
        self.y = lax.axis_index("ch")
        self.core = self.me % 2
        self.chip = self.me // 2
        self.z = self.chip // xs
        self.x = self.chip % xs
        self.twin = self.me + 1 - 2 * self.core

    def at(self, dz, dx):
        return (self.z + dz + self.zs) % self.zs * self.xs + (self.x + dx + self.xs) % self.xs


def greet(place, count, ys):
    barrier = pltpu.get_barrier_semaphore()

    def tell(**where):
        pl.semaphore_signal(barrier, inc=1, device_id=where, device_id_type=pl.DeviceIdType.MESH)

    def shard(i, carry):
        tell(ctx=(place.me + i) % count)
        return carry

    lax.fori_loop(1, count, shard, 0)
    for dy in range(1, ys):
        other = (place.y + dy) % ys
        tell(ch=other)
        for dz in REACH:

            def chip(i, carry):
                tell(ctx=place.at(dz, i) * 2 + place.core, ch=other)
                return carry

            lax.fori_loop(0 if dz else 1, place.xs, chip, 0)
    extra = (ys - 1) * (len(REACH) * place.xs - 1)
    return lambda: pl.semaphore_wait(barrier, count - 1 + ys - 1 + extra)


REACH = (0, 1, -1, 4)
ORDER = (4, 0, 2, 6, 1, 7, 3, 5)


def shift_of(y):
    return jnp.where(y == 1, 2, jnp.where(y == 3, -2, 0))


def nearest(d, y):
    if d in (2, 3):
        return 3, d - 2, (y + 1) % 4 + 4 * (d == 3)
    if d in (5, 6):
        return 1, d - 6, (y + 3) % 4 + 4 * (d == 5)
    return jnp.where((y == 0) | (y == 3), 0, 2), {0: 0, 4: 4, 1: 1, 7: -1}[d], 2 * (0, 4, 1, 7).index(d) + y % 2


def came_from(q, odd_group, y):
    turned = y % 2 == 1
    group = 2 * q + odd_group
    moved = jnp.where(turned, (y - 2) * (q >= 2), (0, 4, 1, -1)[q])
    return moved, jnp.where(turned, (group % 4 + y) % 4, (y + 3 * odd_group) % 4)


def offsets(q, half, j):
    if half == 0:
        return 4 - q, j
    return (4 + q if q else 0), (j + 1) % 4


def each(q, act):
    for half in range(2):

        def one(j, carry):
            dz, dx = offsets(q, half, j)
            act(q * 8 + half * 4 + j, dz, dx)
            return carry

        lax.fori_loop(0, 3 if q == 0 and half == 1 else 4, one, 0)


def split(refs, far, outs, conv, moe, sems):
    refs = list(refs)
    cut = [refs[:far], refs[far : far + outs]]
    rest = refs[far + outs :]
    first = rest[:conv]
    cut.append((first[: far + 1], *first[far + 1 :]))
    cut.append(rest[conv : conv + moe])
    cut.append(rest[conv + moe :])
    return cut


def layer_kernel(
    signal, taps, skip, gain, router_t, routes_t, gate_hbm, *rest
):
    place = Place()
    me, core, chip, y = place.me, place.core, place.chip, place.y
    (
        far, (mixed_out, out),
        (near, packed, fields, re_ref, im_ref, conv_out, conv_in, mixed, full),
        (send, here, got, twin_got, part, twin_part, summed, back, moe, landed, own, stage_up, stage_down, up_ref, down_ref),
        (far_sem, local_sem, conv_sem, xs_sem, xr_sem, send_sem, got_sem, fs_sem, fr_sem, ps_sem, pr_sem,
         rs_sem, back_sem, ms_sem, mr_sem, zs_sem, zr_sem, ys_sem, yr_sem, keep_sem),
    ) = split(rest, 8, 2, 17, 15, 20)
    shards, width_ch = 64, signal.shape[1]
    chans = width_ch // shards
    ready = greet(place, shards, 4)
    fetches = [
        pltpu.make_async_copy(a, b, far_sem.at[i]) for i, (a, b) in enumerate(zip((gate_hbm, *far), near))
    ]
    for fetch in fetches:
        fetch.start()
    gate, tables, own_up, own_down = near[0], near[1:7], near[7], near[8]
    wide, deep = own_up.shape[0] // 4, own_down.shape[0] // 4

    def quarter(k):
        return pl.ds(pl.multiple_of(k * wide, wide), wide), pl.ds(pl.multiple_of(k * deep, deep), deep)

    def step_along_z(side):
        up_rows, down_rows = quarter(y)
        to = place.at(2 - 4 * side, 0) * 2 + core
        return (
            remote(own_up.at[up_rows], stage_up.at[side], zs_sem.at[side, 0], zr_sem.at[side, 0], ctx=to),
            remote(own_down.at[down_rows], stage_down.at[side], zs_sem.at[side, 1], zr_sem.at[side, 1], ctx=to),
        )

    def step_along_y(side):
        up_rows, down_rows = quarter(y)
        to = 1 + 2 * side
        return (
            remote(stage_up.at[side], up_ref.at[up_rows], ys_sem.at[side, 0], yr_sem.at[0], ch=to),
            remote(stage_down.at[side], down_ref.at[down_rows], ys_sem.at[side, 1], yr_sem.at[1], ch=to),
        )

    def stays(side):
        up_rows, down_rows = quarter(y)
        return (
            pltpu.make_async_copy(stage_up.at[side], up_ref.at[up_rows], keep_sem.at[0]),
            pltpu.make_async_copy(stage_down.at[side], down_ref.at[down_rows], keep_sem.at[1]),
        )

    def whole_weights():
        return (
            pltpu.make_async_copy(own_up, up_ref, keep_sem.at[0]),
            pltpu.make_async_copy(own_down, down_ref, keep_sem.at[1]),
        )

    def act(copies, what):
        for copy in copies:
            getattr(copy, what)()

    packed[...] = pack(signal[...], taps[...], shards, 2 * chans).reshape(packed.shape).astype(bf16)
    here[...] = slots_of(routes_t[...], router_t.shape[0])
    ready()

    def spread_out(source, target, ss, rs):
        def both(to):
            for side in range(2):
                where = to * 2 + side
                remote(source.at[where], target.at[me], ss, rs, ctx=where).start()

        for q in range(4):
            each(q, lambda slot, dz, dx: both(place.at(dz, dx)))
        remote(source.at[place.twin], target.at[me], ss, rs, ctx=place.twin).start()
        stay = pltpu.make_async_copy(source.at[me], target.at[me], local_sem.at[2])
        stay.start()
        most = pl.ds(0, shards - 1)
        whole = remote(source.at[most], target.at[most], ss, rs, ctx=place.twin)
        whole.wait_recv()
        stay.wait()
        return whole

    whole = spread_out(packed, fields, conv_sem.at[0], conv_sem.at[1])
    for fetch in fetches:
        fetch.wait()
    act((*step_along_z(0), *step_along_z(1)), "start")
    data = fields[...].astype(f32).reshape(shards * 2 * chans, -1).astype(bf16)
    total = convolve(data, tables, re_ref, im_ref, shards, chans)
    conv_out[...] = total.reshape(conv_out.shape).astype(bf16)
    whole_back = spread_out(conv_out, conv_in, conv_sem.at[2], conv_sem.at[3])
    whole.wait_send()
    data = conv_in[...].astype(f32).reshape(shards * 2 * chans, -1).astype(bf16)
    for side in range(2):
        conv = unpack(data, side, 2 * chans)
        count = conv.shape[0]
        span = slice(side * count, (side + 1) * count)
        sig = signal[span, :].astype(f32)
        value = (gate[span, :].astype(f32) * (conv + skip[...] * sig)).astype(bf16)
        mixed_out[span, :] = value
        for k in range(2 * side, 2 * side + 2):
            mixed[k] = value[(k % 2) * (count // 2) : (k % 2 + 1) * (count // 2)]

            @pl.when(y != k)
            def _():
                remote(mixed.at[k], full.at[y], xs_sem, xr_sem, ch=k).start()

    full[y] = mixed[y]
    act((*step_along_z(0), *step_along_z(1)), "wait")
    for side in range(2):
        pl.when(y != 1 + 2 * side)(lambda: act(step_along_y(side), "start"))
        pl.when(y == 1 + 2 * side)(lambda: act(stays(side), "start"))
    pl.when(y % 2 == 0)(lambda: act(whole_weights(), "start"))
    trio = pl.ds(0, 3)
    quarters = remote(mixed.at[trio], full.at[trio], xs_sem, xr_sem, ch=(y + 1) % 4)
    quarters.wait_recv()
    normed = normalize(jnp.concatenate([full[k] for k in range(4)], axis=1).astype(f32), gain[...])
    send[...] = dot(here[...], normed).astype(bf16).reshape(send.shape)
    chunk = 8
    rows = chunk * CAP
    for d in ORDER:
        plane, moved, group = nearest(d, y)

        def dispatch(j, carry):
            dx = (j + 1 - group % 2) % 4
            slot = group // 2 * chunk + (1 - group % 2) * 4 + j

            @pl.when(jnp.logical_or(group != 0, dx != 0))
            def _():
                remote(
                    send.at[place.at(d, dx)], got.at[slot], send_sem, got_sem.at[group // 2],
                    ctx=place.at(moved, dx) * 2 + core, ch=plane,
                ).start()

            return carry

        lax.fori_loop(0, 4, dispatch, 0)
    home = place.at(-shift_of(y), 0)
    keep = pltpu.make_async_copy(send.at[home], got.at[7], local_sem.at[0])
    keep.start()
    keep_back = pltpu.make_async_copy(summed.at[7], back.at[home], local_sem.at[1])
    hi, lo = gates_of(normed, router_t[...], here[...])
    quarters.wait_send()
    whole_back.wait_send()

    for side in range(2):
        pl.when(y != 1 + 2 * side)(lambda: act(step_along_y(side), "wait_send"))
        pl.when(y == 1 + 2 * side)(lambda: act(stays(side), "wait"))
    pl.when(y % 2 == 0)(lambda: act(whole_weights(), "wait"))

    @pl.when(y % 2 == 1)
    def _():
        three = pl.ds(0, 3 * wide), pl.ds(0, 3 * deep)
        remote(own_up.at[three[0]], up_ref.at[three[0]], ys_sem.at[0, 0], yr_sem.at[0], ch=0).wait_recv()
        remote(own_down.at[three[1]], down_ref.at[three[1]], ys_sem.at[0, 1], yr_sem.at[1], ch=0).wait_recv()

    def mlp(block):
        x = block.reshape(rows, block.shape[-1])
        hidden = jax.nn.gelu(dot(x, up_ref[...]), approximate=True).astype(bf16)
        return dot(hidden, down_ref[...])

    for q in range(4):
        slots = pl.ds(q * chunk, chunk)
        came = pl.ds(q * chunk, 7) if q == 0 else slots
        remote(send.at[came], got.at[came], send_sem, got_sem.at[q], ctx=me).wait_recv()
        if q == 0:
            keep.wait()
        share = remote(got.at[slots], twin_got.at[slots], fs_sem.at[q], fr_sem.at[q], ctx=place.twin)
        share.start()
        own[...] = mlp(got[slots])
        share.wait_recv()
        part[slots] = mlp(twin_got[slots]).astype(bf16).reshape(chunk, CAP, -1)
        give = remote(part.at[slots], twin_part.at[slots], ps_sem.at[q], pr_sem.at[q], ctx=place.twin)
        give.start()
        give.wait_recv()
        total = own[...].reshape(chunk, CAP, -1) + twin_part[slots].astype(f32)
        summed[slots] = total.astype(bf16)

        for odd_group in range(2):
            moved, sender = came_from(q, odd_group, y)

            def give_back(j, carry):
                dx = (j + 1 - odd_group) % 4
                slot = q * chunk + (1 - odd_group) * 4 + j
                to = place.at(-moved, -dx) * 2 + core
                remote(summed.at[slot], back.at[home], rs_sem, back_sem, ctx=to, ch=sender).start()
                return carry

            lax.fori_loop(0, 3 if q == 0 and odd_group == 0 else 4, give_back, 0)
        if q == 0:
            keep_back.start()
        share.wait_send()
        give.wait_send()
    keep_back.wait()
    others = pl.ds(0, 31)
    remote(summed.at[others], back.at[others], rs_sem, back_sem, ctx=me).wait_recv()
    gathered = back[...].reshape(32 * CAP, -1)
    result = (dot(hi, gathered) + dot(lo, gathered)).astype(bf16)
    width = moe.shape[-1]
    for k in range(4):
        moe[k] = result[:, k * width : (k + 1) * width]
    copies = []
    for dy in range(1, 4):
        to = (y + dy) % 4
        copies.append(remote(moe.at[to], landed.at[y], ms_sem.at[dy - 1], mr_sem.at[dy - 1], ch=to))
        copies[-1].start()
    landed[y] = moe[y]
    for copy in copies:
        copy.wait()
    out[...] = landed[...].reshape(out.shape)
    remote(send.at[others], got.at[others], send_sem, got_sem.at[0], ctx=me).wait_send()
    remote(summed.at[others], back.at[others], rs_sem, back_sem, ctx=me).wait_send()


def call(kernel, out_shape, *args, scratch=()):
    return pl.pallas_call(
        kernel,
        out_shape=out_shape,
        in_specs=[pl.BlockSpec(memory_space=pltpu.VMEM)] * len(args),
        out_specs=jax.tree.map(lambda _: pl.BlockSpec(memory_space=pltpu.VMEM), out_shape),
        scratch_shapes=list(scratch),
    )(*args)


def body(signal, gate_v, taps, skip, norm_gain, router, w_up, w_down, routes):
    tok_dev, ch_dev = signal.shape
    shards = lax.axis_size("ctx")
    groups = lax.axis_size("ch")
    chans = ch_dev // shards
    experts = router.shape[1]
    width = norm_gain.shape[0]
    rows = tok_dev // groups
    hidden = w_up.shape[2]
    shape = jax.ShapeDtypeStruct
    far = (*dft_constants(shards, tok_dev, chans), w_up[0], w_down[0])
    blocks = (experts, CAP, width)
    dma = pltpu.SemaphoreType.DMA
    vmem = pltpu.VMEM
    here = pl.BlockSpec(memory_space=vmem)
    there = pl.BlockSpec(memory_space=pl.ANY)
    local = shape((tok_dev, ch_dev), bf16)
    mixed, moe_out = pl.pallas_call(
        layer_kernel,
        out_shape=(local, local),
        in_specs=[here] * 6 + [there] * (1 + len(far)),
        out_specs=(here, here),
        scratch_shapes=[vmem(gate_v.shape, gate_v.dtype)]
        + [vmem(a.shape, a.dtype) for a in far]
        + [vmem((shards, 2 * chans, tok_dev), bf16)] * 2
        + [vmem((2 * chans * shards, tok_dev), bf16)] * 2
        + [vmem((shards, 2 * chans, tok_dev // 2), bf16)] * 2
        + [vmem((groups, rows, ch_dev), bf16)] * 2
        + [vmem(blocks, bf16)]
        + [vmem((experts * CAP, rows), bf16)]
        + [vmem(blocks, bf16)] * 6
        + [vmem((groups, rows, ch_dev), bf16)] * 2
        + [vmem((rows, width), f32)]
        + [vmem((2, width // 4, hidden), bf16), vmem((2, hidden // 4, width), bf16)]
        + [vmem((width, hidden), bf16), vmem((hidden, width), bf16)]
        + [dma((9,)), dma((3,)), dma((4,)), dma, dma, dma]
        + [dma((4,))] * 5
        + [dma, dma, dma((3,)), dma((3,))]
        + [dma((2, 2))] * 3
        + [dma((2,))] * 2,
        compiler_params=pltpu.CompilerParams(collective_id=0, has_side_effects=True),
    )(signal, taps, skip[None, :], norm_gain[None, :], router.T, routes.T, gate_v, *far)
    return (mixed, moe_out)


def solution(mesh):
    in_specs = (
        P("ctx", "ch"),
        P("ctx", "ch"),
        P("ctx", "ch"),
        P("ch"),
        P(),
        P(),
        P("ctx", None, None),
        P("ctx", None, None),
        P(("ctx", "ch"), None),
    )
    out_specs = (P("ctx", "ch"), P("ctx", "ch"))
    return jax.shard_map(body, mesh=mesh, in_specs=in_specs, out_specs=out_specs, check_vma=False)
```

```python
import math

import jax
import jax.numpy as jnp
import numpy as np
from jax import lax
from jax.experimental import pallas as pl
from jax.experimental.pallas import tpu as pltpu
from jax.sharding import PartitionSpec as P

CAP = 16
bf16 = jnp.bfloat16
f32 = jnp.float32


def dft_constants(shards, tok, chans):
    total = shards * tok
    fields = 2 * chans
    row = np.arange(shards)
    col = np.arange(tok)
    outer = 2.0 * np.pi * row[None, :] * (row[:, None] + 0.25) / shards
    first = np.concatenate([np.cos(outer), -np.sin(outer)], axis=0)
    first = np.repeat(first, fields, axis=1)
    last = np.concatenate([np.cos(outer.T), -np.sin(outer.T)], axis=1) / total
    last = np.repeat(last, fields, axis=0)
    turn = 2.0 * np.pi * (row[:, None] + 0.25) * col[None, :] / total
    inner = 2.0 * np.pi * ((col[:, None] * col[None, :]) % tok) / tok
    as16 = lambda a: jnp.asarray(a.astype(np.float32), bf16)
    as32 = lambda a: jnp.asarray(a.astype(np.float32))
    return (
        as16(first),
        as32(np.cos(turn)),
        as32(-np.sin(turn)),
        as16(np.cos(inner)),
        as16(np.sin(inner)),
        as16(last),
    )


def dot(a, b):
    return jnp.dot(a, b, preferred_element_type=f32)


def iota(shape, axis):
    return lax.broadcasted_iota(jnp.int32, shape, axis)


def one_hot(mask):
    return mask.astype(f32).astype(bf16)


def contract(a, b, axis_a, axis_b):
    return lax.dot_general(a, b, (((axis_a,), (axis_b,)), ((), ())), preferred_element_type=f32)


def pack(signal, taps, shards, fields):
    chans = fields // 2
    shape = (shards * fields, signal.shape[1])
    row, chan = iota(shape, 0), iota(shape, 1)
    field = row % fields
    mine = row // fields * chans + field % chans == chan
    sig = contract(one_hot(mine & (field < chans)), signal, 1, 1)
    tap = contract(one_hot(mine & (field >= chans)), taps.astype(bf16), 1, 1)
    return sig + tap


def convolve(data, tables, re_ref, im_ref, shards, chans):
    first, tr, ti, cos, sin, last = (table[...] for table in tables)
    fields = 2 * chans
    tok = data.shape[1]
    lane = iota(first.shape, 1) % fields
    for field in range(fields):
        g = dot(jnp.where(lane == field, first, jnp.zeros_like(first)), data)
        g_re, g_im = g[:shards], g[shards:]
        rows = pl.ds(field * shards, shards)
        re_ref[rows, :] = (g_re * tr - g_im * ti).astype(bf16)
        im_ref[rows, :] = (g_re * ti + g_im * tr).astype(bf16)
    re, im = re_ref[...], im_ref[...]
    x_re = dot(re, cos) + dot(im, sin)
    x_im = dot(im, cos) - dot(re, sin)
    half = chans * shards
    p_re = (x_re[:half] * x_re[half:] - x_im[:half] * x_im[half:]).astype(bf16)
    p_im = (x_re[:half] * x_im[half:] + x_im[:half] * x_re[half:]).astype(bf16)
    g_re = dot(p_re, cos) - dot(p_im, sin)
    g_im = dot(p_im, cos) + dot(p_re, sin)
    row = iota(last.shape, 0) % fields
    total = jnp.zeros((shards * fields, tok // 2), f32)
    for chan in range(chans):
        rows = slice(chan * shards, (chan + 1) * shards)
        a = (g_re[rows] * tr + g_im[rows] * ti).astype(bf16)
        b = (g_im[rows] * tr - g_re[rows] * ti).astype(bf16)
        both = jnp.concatenate([a, b], axis=0)
        for side in range(2):
            table = jnp.where(row == side * chans + chan, last, jnp.zeros_like(last))
            total += dot(table, both[:, side * (tok // 2) : (side + 1) * (tok // 2)])
    return total


def unpack(data, side, fields):
    chans = fields // 2
    shape = (data.shape[0], data.shape[0] // fields * chans)
    row, chan = iota(shape, 0), iota(shape, 1)
    field = row % fields
    mine = (row // fields * chans + field % chans == chan) & (field // chans == side)
    return contract(data, one_hot(mine), 0, 0)


def slots_of(routes_t, experts):
    count = routes_t.shape[1]
    slots = experts * CAP
    ids = iota((experts, count), 0)
    named = one_hot((routes_t[0:1, :] == ids) | (routes_t[1:2, :] == ids))
    rank = dot(named, one_hot(iota((count, count), 0) < iota((count, count), 1))).astype(bf16)
    spread = one_hot(iota((slots, experts), 0) // CAP == iota((slots, experts), 1))
    slot = (iota((slots, count), 0) % CAP).astype(f32)
    return one_hot((dot(spread, named) > 0.5) & (dot(spread, rank) == slot))


def normalize(x, gain):
    scale = lax.rsqrt(jnp.mean(x * x, axis=-1, keepdims=True) + 1e-05)
    return (x * scale * gain).astype(bf16)


def gates_of(normed, router_t, here):
    count = normed.shape[0]
    experts = router_t.shape[0]
    slots = experts * CAP
    logits = lax.dot_general(
        router_t,
        normed.astype(f32),
        (((1,), (1,)), ((), ())),
        precision=lax.Precision.HIGHEST,
        preferred_element_type=f32,
    )
    gates = jax.nn.sigmoid(logits)
    high = gates.astype(bf16)
    low = (gates - high.astype(f32)).astype(bf16)
    spread = one_hot(iota((slots, experts), 0) // CAP == iota((slots, experts), 1))
    turn = one_hot(iota((count, count), 0) == iota((count, count), 1))
    chosen = here > 0.5
    parts = (jnp.where(chosen, dot(spread, part), 0.0).astype(bf16) for part in (high, low))
    return tuple(contract(turn, part, 1, 1).astype(bf16) for part in parts)


def remote(src, dst, send_sem, recv_sem, **where):
    return pltpu.make_async_remote_copy(
        src_ref=src,
        dst_ref=dst,
        send_sem=send_sem,
        recv_sem=recv_sem,
        device_id=where,
        device_id_type=pl.DeviceIdType.MESH,
    )


class Place:
    def __init__(self, zs=8, xs=4):
        self.zs, self.xs = zs, xs
        self.me = lax.axis_index("ctx")
        self.y = lax.axis_index("ch")
        self.core = self.me % 2
        self.chip = self.me // 2
        self.z = self.chip // xs
        self.x = self.chip % xs
        self.twin = self.me + 1 - 2 * self.core

    def at(self, dz, dx):
        return (self.z + dz + self.zs) % self.zs * self.xs + (self.x + dx + self.xs) % self.xs


def greet(place, count, ys):
    barrier = pltpu.get_barrier_semaphore()

    def tell(**where):
        pl.semaphore_signal(barrier, inc=1, device_id=where, device_id_type=pl.DeviceIdType.MESH)

    def shard(i, carry):
        tell(ctx=(place.me + i) % count)
        return carry

    lax.fori_loop(1, count, shard, 0)
    for dy in range(1, ys):
        tell(ch=(place.y + dy) % ys)
    return lambda: pl.semaphore_wait(barrier, count - 1 + ys - 1)


def offsets(q, half, j):
    if half == 0:
        return 4 - q, j
    return (4 + q if q else 0), (j + 1) % 4


def each(q, act):
    for half in range(2):

        def one(j, carry):
            dz, dx = offsets(q, half, j)
            act(q * 8 + half * 4 + j, dz, dx)
            return carry

        lax.fori_loop(0, 3 if q == 0 and half == 1 else 4, one, 0)


def split(refs, counts):
    refs = list(refs)
    return [[refs.pop(0) for _ in range(count)] for count in counts]


def publish_kernel(a_ref, b_ref, a_out, b_out):
    a_out[...] = a_ref[...]
    b_out[...] = b_ref[...]


def layer_kernel(
    skip, gain, routes_t, *rest
):
    place = Place()
    me, core, chip, y = place.me, place.core, place.chip, place.y
    (
        far, (mixed_out, out),
        near, (packed, fields, re_ref, im_ref, conv_out, conv_in, mixed, full),
        (send, here, got, summed, back, moe, landed, ups, downs),
        (far_sem, local_sem, conv_sem, xs_sem, xr_sem, send_sem, got_sem, ws_sem, wr_sem,
         rs_sem, back_sem, ms_sem, mr_sem),
    ) = split(rest, (12, 2, 10, 8, 9, 13))
    shards, width_ch = 64, near[0].shape[1]
    chans = width_ch // shards
    ready = greet(place, shards, 4)
    near = (*near, ups.at[0], downs.at[0])
    fetches = [pltpu.make_async_copy(a, b, far_sem.at[i]) for i, (a, b) in enumerate(zip(far, near))]
    for fetch in fetches:
        fetch.start()
    signal, taps, gate, router_t, tables = near[0], near[1], near[2], near[3], near[4:10]
    fetches[0].wait()
    fetches[1].wait()
    packed[...] = pack(signal[...], taps[...], shards, 2 * chans).reshape(packed.shape).astype(bf16)
    here[...] = slots_of(routes_t[...], router_t.shape[0])
    for fetch in fetches[2:]:
        fetch.wait()
    ready()

    def spread_out(source, target, ss, rs):
        def both(to):
            for side in range(2):
                where = to * 2 + side
                remote(source.at[where], target.at[me], ss, rs, ctx=where).start()

        for q in range(4):
            each(q, lambda slot, dz, dx: both(place.at(dz, dx)))
        remote(source.at[place.twin], target.at[me], ss, rs, ctx=place.twin).start()
        stay = pltpu.make_async_copy(source.at[me], target.at[me], local_sem.at[2])
        stay.start()
        most = pl.ds(0, shards - 1)
        whole = remote(source.at[most], target.at[most], ss, rs, ctx=place.twin)
        whole.wait_recv()
        stay.wait()
        return whole

    swaps = [
        remote(both.at[0], both.at[1], ws_sem.at[i], wr_sem.at[i], ctx=place.twin)
        for i, both in enumerate((ups, downs))
    ]
    whole = spread_out(packed, fields, conv_sem.at[0], conv_sem.at[1])
    for swap in swaps:
        swap.start()
    data = fields[...].astype(f32).reshape(shards * 2 * chans, -1).astype(bf16)
    total = convolve(data, tables, re_ref, im_ref, shards, chans)
    conv_out[...] = total.reshape(conv_out.shape).astype(bf16)
    whole_back = spread_out(conv_out, conv_in, conv_sem.at[2], conv_sem.at[3])
    whole.wait_send()
    data = conv_in[...].astype(f32).reshape(shards * 2 * chans, -1).astype(bf16)
    for side in range(2):
        conv = unpack(data, side, 2 * chans)
        count = conv.shape[0]
        span = slice(side * count, (side + 1) * count)
        sig = signal[span, :].astype(f32)
        value = (gate[span, :].astype(f32) * (conv + skip[...] * sig)).astype(bf16)
        mixed_out[span, :] = value
        for k in range(2 * side, 2 * side + 2):
            mixed[k] = value[(k % 2) * (count // 2) : (k % 2 + 1) * (count // 2)]

            @pl.when(y != k)
            def _():
                remote(mixed.at[k], full.at[y], xs_sem, xr_sem, ch=k).start()

    full[y] = mixed[y]
    trio = pl.ds(0, 3)
    quarters = remote(mixed.at[trio], full.at[trio], xs_sem, xr_sem, ch=(y + 1) % 4)
    quarters.wait_recv()
    normed = normalize(jnp.concatenate([full[k] for k in range(4)], axis=1).astype(f32), gain[...])
    send[...] = dot(here[...], normed).astype(bf16).reshape(send.shape)
    chunk = 8
    rows = chunk * CAP
    for q in range(4):

        def dispatch(slot, dz, dx):
            to = place.at(dz, dx)
            remote(send.at[to], got.at[slot], send_sem, got_sem.at[q], ctx=to * 2 + core).start()

        each(q, dispatch)
    keep = pltpu.make_async_copy(send.at[chip], got.at[7], local_sem.at[0])
    keep.start()
    keep_back = pltpu.make_async_copy(summed.at[7], back.at[chip], local_sem.at[1])
    hi, lo = gates_of(normed, router_t[...], here[...])
    quarters.wait_send()
    whole_back.wait_send()

    for swap in swaps:
        swap.wait()
    for q in range(4):
        slots = pl.ds(q * chunk, chunk)
        came = pl.ds(q * chunk, 7) if q == 0 else slots
        remote(send.at[came], got.at[came], send_sem, got_sem.at[q], ctx=me).wait_recv()
        if q == 0:
            keep.wait()
        x = got[slots].reshape(rows, -1)
        total = None
        for half in range(2):
            hidden = jax.nn.gelu(dot(x, ups[half]), approximate=True).astype(bf16)
            part = dot(hidden, downs[half])
            total = part if half == 0 else total + part
        summed[slots] = total.astype(bf16).reshape(chunk, CAP, -1)

        def give_back(slot, dz, dx):
            to = place.at(-dz, -dx)
            remote(summed.at[slot], back.at[chip], rs_sem, back_sem, ctx=to * 2 + core).start()

        each(q, give_back)
        if q == 0:
            keep_back.start()
    keep_back.wait()
    others = pl.ds(0, 31)
    remote(summed.at[others], back.at[others], rs_sem, back_sem, ctx=me).wait_recv()
    gathered = back[...].reshape(32 * CAP, -1)
    result = (dot(hi, gathered) + dot(lo, gathered)).astype(bf16)
    width = moe.shape[-1]
    for k in range(4):
        moe[k] = result[:, k * width : (k + 1) * width]
    copies = []
    for dy in range(1, 4):
        to = (y + dy) % 4
        copies.append(remote(moe.at[to], landed.at[y], ms_sem.at[dy - 1], mr_sem.at[dy - 1], ch=to))
        copies[-1].start()
    landed[y] = moe[y]
    for copy in copies:
        copy.wait()
    out[...] = landed[...].reshape(out.shape)
    remote(send.at[others], got.at[others], send_sem, got_sem.at[0], ctx=me).wait_send()
    remote(summed.at[others], back.at[others], rs_sem, back_sem, ctx=me).wait_send()


def call(kernel, out_shape, *args, scratch=()):
    return pl.pallas_call(
        kernel,
        out_shape=out_shape,
        in_specs=[pl.BlockSpec(memory_space=pltpu.VMEM)] * len(args),
        out_specs=jax.tree.map(lambda _: pl.BlockSpec(memory_space=pltpu.VMEM), out_shape),
        scratch_shapes=list(scratch),
    )(*args)


def body(signal, gate_v, taps, skip, norm_gain, router, w_up, w_down, routes):
    tok_dev, ch_dev = signal.shape
    shards = lax.axis_size("ctx")
    groups = lax.axis_size("ch")
    chans = ch_dev // shards
    experts = router.shape[1]
    width = norm_gain.shape[0]
    rows = tok_dev // groups
    shape = jax.ShapeDtypeStruct
    far = (
        signal, taps, gate_v, router.T, *dft_constants(shards, tok_dev, chans), w_up[0], w_down[0],
    )
    hidden = w_up.shape[2]
    blocks = (experts, CAP, width)
    dma = pltpu.SemaphoreType.DMA
    vmem = pltpu.VMEM
    here = pl.BlockSpec(memory_space=vmem)
    there = pl.BlockSpec(memory_space=pl.ANY)
    local = shape((tok_dev, ch_dev), bf16)
    results = pl.pallas_call(
        layer_kernel,
        out_shape=(local, local),
        in_specs=[here] * 3 + [there] * len(far),
        out_specs=(here, here),
        scratch_shapes=[vmem(a.shape, a.dtype) for a in far[:-2]]
        + [vmem((shards, 2 * chans, tok_dev), bf16)] * 2
        + [vmem((2 * chans * shards, tok_dev), bf16)] * 2
        + [vmem((shards, 2 * chans, tok_dev // 2), bf16)] * 2
        + [vmem((groups, rows, ch_dev), bf16)] * 2
        + [vmem(blocks, bf16)]
        + [vmem((experts * CAP, rows), bf16)]
        + [vmem(blocks, bf16)] * 3
        + [vmem((groups, rows, ch_dev), bf16)] * 2
        + [vmem((2, width, hidden), bf16), vmem((2, hidden, width), bf16)]
        + [dma((12,)), dma((3,)), dma((4,)), dma, dma, dma]
        + [dma((4,)), dma((2,)), dma((2,))]
        + [dma, dma, dma((3,)), dma((3,))],
        compiler_params=pltpu.CompilerParams(collective_id=0, has_side_effects=True),
    )(skip[None, :], norm_gain[None, :], routes.T, *far)
    return tuple(
        pl.pallas_call(
            publish_kernel,
            out_shape=(local, local),
            in_specs=[here] * 2,
            out_specs=(here, here),
        )(*results)
    )


def solution(mesh):
    in_specs = (
        P("ctx", "ch"),
        P("ctx", "ch"),
        P("ctx", "ch"),
        P("ch"),
        P(),
        P(),
        P("ctx", None, None),
        P("ctx", None, None),
        P(("ctx", "ch"), None),
    )
    out_specs = (P("ctx", "ch"), P("ctx", "ch"))
    return jax.shard_map(body, mesh=mesh, in_specs=in_specs, out_specs=out_specs, check_vma=False)
```

```python
import math

import jax
import jax.numpy as jnp
import numpy as np
from jax import lax
from jax.experimental import pallas as pl
from jax.experimental.pallas import tpu as pltpu
from jax.sharding import PartitionSpec as P

CAP = 16
bf16 = jnp.bfloat16
f32 = jnp.float32


def dft_constants(shards, tok, chans):
    total = shards * tok
    fields = 2 * chans
    row = np.arange(shards)
    col = np.arange(tok)
    outer = 2.0 * np.pi * row[None, :] * (row[:, None] + 0.25) / shards
    first = np.concatenate([np.cos(outer), -np.sin(outer)], axis=0)
    first = np.repeat(first, fields, axis=1)
    last = np.concatenate([np.cos(outer.T), -np.sin(outer.T)], axis=1) / total
    last = np.repeat(last, fields, axis=0)
    turn = 2.0 * np.pi * (row[:, None] + 0.25) * col[None, :] / total
    inner = 2.0 * np.pi * ((col[:, None] * col[None, :]) % tok) / tok
    as16 = lambda a: jnp.asarray(a.astype(np.float32), bf16)
    as32 = lambda a: jnp.asarray(a.astype(np.float32))
    return (
        as16(first),
        as32(np.cos(turn)),
        as32(-np.sin(turn)),
        as16(np.cos(inner)),
        as16(np.sin(inner)),
        as16(last),
    )


def dot(a, b):
    return jnp.dot(a, b, preferred_element_type=f32)


def iota(shape, axis):
    return lax.broadcasted_iota(jnp.int32, shape, axis)


def one_hot(mask):
    return mask.astype(f32).astype(bf16)


def contract(a, b, axis_a, axis_b):
    return lax.dot_general(a, b, (((axis_a,), (axis_b,)), ((), ())), preferred_element_type=f32)


def pack(signal, taps, shards, fields):
    chans = fields // 2
    shape = (shards * fields, signal.shape[1])
    row, chan = iota(shape, 0), iota(shape, 1)
    field = row % fields
    mine = row // fields * chans + field % chans == chan
    sig = contract(one_hot(mine & (field < chans)), signal, 1, 1)
    tap = contract(one_hot(mine & (field >= chans)), taps.astype(bf16), 1, 1)
    return sig + tap


def convolve(data, tables, re_ref, im_ref, shards, chans):
    first, tr, ti, cos, sin, last = (table[...] for table in tables)
    fields = 2 * chans
    tok = data.shape[1]
    lane = iota(first.shape, 1) % fields
    for field in range(fields):
        g = dot(jnp.where(lane == field, first, jnp.zeros_like(first)), data)
        g_re, g_im = g[:shards], g[shards:]
        rows = pl.ds(field * shards, shards)
        re_ref[rows, :] = (g_re * tr - g_im * ti).astype(bf16)
        im_ref[rows, :] = (g_re * ti + g_im * tr).astype(bf16)
    re, im = re_ref[...], im_ref[...]
    x_re = dot(re, cos) + dot(im, sin)
    x_im = dot(im, cos) - dot(re, sin)
    half = chans * shards
    p_re = (x_re[:half] * x_re[half:] - x_im[:half] * x_im[half:]).astype(bf16)
    p_im = (x_re[:half] * x_im[half:] + x_im[:half] * x_re[half:]).astype(bf16)
    g_re = dot(p_re, cos) - dot(p_im, sin)
    g_im = dot(p_im, cos) + dot(p_re, sin)
    row = iota(last.shape, 0) % fields
    total = jnp.zeros((shards * fields, tok // 2), f32)
    for chan in range(chans):
        rows = slice(chan * shards, (chan + 1) * shards)
        a = (g_re[rows] * tr + g_im[rows] * ti).astype(bf16)
        b = (g_im[rows] * tr - g_re[rows] * ti).astype(bf16)
        both = jnp.concatenate([a, b], axis=0)
        for side in range(2):
            table = jnp.where(row == side * chans + chan, last, jnp.zeros_like(last))
            total += dot(table, both[:, side * (tok // 2) : (side + 1) * (tok // 2)])
    return total


def unpack(data, side, fields):
    chans = fields // 2
    shape = (data.shape[0], data.shape[0] // fields * chans)
    row, chan = iota(shape, 0), iota(shape, 1)
    field = row % fields
    mine = (row // fields * chans + field % chans == chan) & (field // chans == side)
    return contract(data, one_hot(mine), 0, 0)


def slots_of(routes_t, experts):
    count = routes_t.shape[1]
    slots = experts * CAP
    ids = iota((experts, count), 0)
    named = one_hot((routes_t[0:1, :] == ids) | (routes_t[1:2, :] == ids))
    rank = dot(named, one_hot(iota((count, count), 0) < iota((count, count), 1))).astype(bf16)
    spread = one_hot(iota((slots, experts), 0) // CAP == iota((slots, experts), 1))
    slot = (iota((slots, count), 0) % CAP).astype(f32)
    return one_hot((dot(spread, named) > 0.5) & (dot(spread, rank) == slot))


def normalize(x, gain):
    scale = lax.rsqrt(jnp.mean(x * x, axis=-1, keepdims=True) + 1e-05)
    return (x * scale * gain).astype(bf16)


def remote(src, dst, send_sem, recv_sem, **where):
    return pltpu.make_async_remote_copy(
        src_ref=src,
        dst_ref=dst,
        send_sem=send_sem,
        recv_sem=recv_sem,
        device_id=where,
        device_id_type=pl.DeviceIdType.MESH,
    )


class Place:
    def __init__(self, zs=8, xs=4):
        self.zs, self.xs = zs, xs
        self.me = lax.axis_index("ctx")
        self.y = lax.axis_index("ch")
        self.core = self.me % 2
        self.chip = self.me // 2
        self.z = self.chip // xs
        self.x = self.chip % xs
        self.twin = self.me + 1 - 2 * self.core

    def at(self, dz, dx):
        return (self.z + dz + self.zs) % self.zs * self.xs + (self.x + dx + self.xs) % self.xs


def greet(place, count, ys):
    barrier = pltpu.get_barrier_semaphore()

    def tell(**where):
        pl.semaphore_signal(barrier, inc=1, device_id=where, device_id_type=pl.DeviceIdType.MESH)

    def shard(i, carry):
        tell(ctx=(place.me + i) % count)
        return carry

    lax.fori_loop(1, count, shard, 0)
    for dy in range(1, ys):
        tell(ch=(place.y + dy) % ys)
    return lambda: pl.semaphore_wait(barrier, count - 1 + ys - 1)


def offsets(q, half, j):
    if half == 0:
        return 4 - q, j
    return (4 + q if q else 0), (j + 1) % 4


def each(q, act):
    for half in range(2):

        def one(j, carry):
            dz, dx = offsets(q, half, j)
            act(q * 8 + half * 4 + j, dz, dx)
            return carry

        lax.fori_loop(0, 3 if q == 0 and half == 1 else 4, one, 0)


def split(refs, counts):
    refs = list(refs)
    return [[refs.pop(0) for _ in range(count)] for count in counts]


def publish_kernel(a_ref, b_ref, a_out, b_out):
    a_out[...] = a_ref[...]
    b_out[...] = b_ref[...]


def layer_kernel(skip, gain, routes_t, *rest):
    place = Place()
    me, core, chip, y = place.me, place.core, place.chip, place.y
    (
        far, (mixed_out, out),
        near, (packed, fields, re_ref, im_ref, conv_out, conv_in, routes_all),
        (send, here, got, summed, back, ups, downs),
        (far_sem, local_sem, conv_sem, xs_sem, xr_sem, send_sem, got_sem, ws_sem, wr_sem, rs_sem, back_sem),
    ) = split(rest, (12, 2, 10, 7, 7, 11))
    shards, width_ch = 64, near[0].shape[1]
    chans = width_ch // shards
    chips, groups, chunk = 32, 4, 8
    ready = greet(place, shards, groups)
    near = (*near, ups.at[0], downs.at[0])
    fetches = [pltpu.make_async_copy(a, b, far_sem.at[i]) for i, (a, b) in enumerate(zip(far, near))]
    for fetch in fetches:
        fetch.start()
    signal, taps, gate, router_t, tables = near[0], near[1], near[2], near[3], near[4:10]
    fetches[0].wait()
    fetches[1].wait()
    packed[...] = pack(signal[...], taps[...], shards, 2 * chans).reshape(packed.shape).astype(bf16)
    routes_all[y] = routes_t[...]
    for fetch in fetches[2:]:
        fetch.wait()
    ready()

    def spread_out(source, target, ss, rs, meanwhile):
        def both(to):
            for side in range(2):
                where = to * 2 + side
                remote(source.at[where], target.at[me], ss, rs, ctx=where).start()

        for q in range(4):
            each(q, lambda slot, dz, dx: both(place.at(dz, dx)))
        remote(source.at[place.twin], target.at[me], ss, rs, ctx=place.twin).start()
        stay = pltpu.make_async_copy(source.at[me], target.at[me], local_sem.at[2])
        stay.start()
        meanwhile()
        most = pl.ds(0, shards - 1)
        whole = remote(source.at[most], target.at[most], ss, rs, ctx=place.twin)
        whole.wait_recv()
        stay.wait()
        return whole

    tells = [
        remote(routes_t, routes_all.at[y], xs_sem.at[dy - 1], xr_sem.at[dy - 1], ch=(y + dy) % groups)
        for dy in range(1, groups)
    ]

    def all_slots():
        for tell in tells:
            tell.wait()
        for k in range(groups):
            here[k] = slots_of(routes_all[k], chips)

    swaps = [
        remote(both.at[0], both.at[1], ws_sem.at[i], wr_sem.at[i], ctx=place.twin)
        for i, both in enumerate((ups, downs))
    ]
    for tell in tells:
        tell.start()
    whole = spread_out(packed, fields, conv_sem.at[0], conv_sem.at[1], all_slots)
    for swap in swaps:
        swap.start()
    data = fields[...].astype(f32).reshape(shards * 2 * chans, -1).astype(bf16)
    total = convolve(data, tables, re_ref, im_ref, shards, chans)
    conv_out[...] = total.reshape(conv_out.shape).astype(bf16)
    whole_back = spread_out(conv_out, conv_in, conv_sem.at[2], conv_sem.at[3], lambda: None)
    data = conv_in[...].astype(f32).reshape(shards * 2 * chans, -1).astype(bf16)
    for side in range(2):
        conv = unpack(data, side, 2 * chans)
        count = conv.shape[0]
        span = slice(side * count, (side + 1) * count)
        sig = signal[span, :].astype(f32)
        value = (gate[span, :].astype(f32) * (conv + skip[...] * sig)).astype(bf16)
        mixed_out[span, :] = value
        for part in range(2):
            k = 2 * side + part
            rows = value[part * (count // 2) : (part + 1) * (count // 2)]
            send[k * chips : (k + 1) * chips] = dot(here[k], rows).astype(bf16).reshape(chips, CAP, width_ch)

    for q in range(4):

        def dispatch(slot, dz, dx):
            to = place.at(dz, dx)
            for k in range(groups):
                remote(
                    send.at[k * chips + to], got.at[y * chips + slot], send_sem, got_sem.at[q],
                    ctx=to * 2 + core, ch=k,
                ).start()

        each(q, dispatch)
        if q == 0:
            for dy in range(1, groups):
                k = (y + dy) % groups
                remote(
                    send.at[k * chips + chip], got.at[y * chips + 7], send_sem, got_sem.at[0], ch=k
                ).start()
    mine = y * chips + chip
    keep = pltpu.make_async_copy(send.at[mine], got.at[y * chips + 7], local_sem.at[0])
    keep.start()
    keep_back = pltpu.make_async_copy(summed.at[y * chips + 7], back.at[mine], local_sem.at[1])
    whole.wait_send()
    whole_back.wait_send()
    for swap in swaps:
        swap.wait()
    column = router_t[pl.ds(chip, 1), :]
    for q in range(4):
        came = pl.ds(0, groups * chunk - (q == 0))
        remote(send.at[came], got.at[came], send_sem, got_sem.at[q], ctx=me).wait_recv()
        if q == 0:
            keep.wait()
        slices = [got[k * chips + q * chunk : k * chips + (q + 1) * chunk] for k in range(groups)]
        x = jnp.concatenate([piece.reshape(chunk * CAP, width_ch) for piece in slices], axis=1)
        normed = normalize(x.astype(f32), gain[...])
        logit = jnp.sum(normed.astype(f32) * column, axis=-1, keepdims=True)
        total = None
        for half in range(2):
            hidden = jax.nn.gelu(dot(normed, ups[half]), approximate=True).astype(bf16)
            part = dot(hidden, downs[half])
            total = part if half == 0 else total + part
        total = (jax.nn.sigmoid(logit) * total).astype(bf16)
        for k in range(groups):
            piece = total[:, k * width_ch : (k + 1) * width_ch].reshape(chunk, CAP, width_ch)
            summed[k * chips + q * chunk : k * chips + (q + 1) * chunk] = piece

        def give_back(slot, dz, dx):
            to = place.at(-dz, -dx) * 2 + core
            for k in range(groups):
                remote(
                    summed.at[k * chips + slot], back.at[mine], rs_sem, back_sem, ctx=to, ch=k
                ).start()

        each(q, give_back)
        if q == 0:
            for dy in range(1, groups):
                k = (y + dy) % groups
                remote(summed.at[k * chips + 7], back.at[mine], rs_sem, back_sem, ch=k).start()
            keep_back.start()
    keep_back.wait()
    others = pl.ds(0, groups * chips - 1)
    remote(summed.at[others], back.at[others], rs_sem, back_sem, ctx=me).wait_recv()
    for k in range(groups):
        slots = back[k * chips : (k + 1) * chips].reshape(chips * CAP, width_ch)
        rows = contract(here[k], slots, 0, 0).astype(bf16)
        out[k * rows.shape[0] : (k + 1) * rows.shape[0], :] = rows
    remote(send.at[others], got.at[others], send_sem, got_sem.at[0], ctx=me).wait_send()
    remote(summed.at[others], back.at[others], rs_sem, back_sem, ctx=me).wait_send()


def body(signal, gate_v, taps, skip, norm_gain, router, w_up, w_down, routes):
    tok_dev, ch_dev = signal.shape
    shards = lax.axis_size("ctx")
    groups = lax.axis_size("ch")
    chans = ch_dev // shards
    experts = router.shape[1]
    width = norm_gain.shape[0]
    rows = tok_dev // groups
    shape = jax.ShapeDtypeStruct
    far = (
        signal, taps, gate_v, router.T, *dft_constants(shards, tok_dev, chans), w_up[0], w_down[0],
    )
    hidden = w_up.shape[2]
    blocks = (groups * experts, CAP, ch_dev)
    dma = pltpu.SemaphoreType.DMA
    vmem = pltpu.VMEM
    here = pl.BlockSpec(memory_space=vmem)
    there = pl.BlockSpec(memory_space=pl.ANY)
    local = shape((tok_dev, ch_dev), bf16)
    results = pl.pallas_call(
        layer_kernel,
        out_shape=(local, local),
        in_specs=[here] * 3 + [there] * len(far),
        out_specs=(here, here),
        scratch_shapes=[vmem(a.shape, a.dtype) for a in far[:-2]]
        + [vmem((shards, 2 * chans, tok_dev), bf16)] * 2
        + [vmem((2 * chans * shards, tok_dev), bf16)] * 2
        + [vmem((shards, 2 * chans, tok_dev // 2), bf16)] * 2
        + [vmem((groups, 2, rows), routes.dtype)]
        + [vmem(blocks, bf16)]
        + [vmem((groups, experts * CAP, rows), bf16)]
        + [vmem(blocks, bf16)] * 3
        + [vmem((2, width, hidden), bf16), vmem((2, hidden, width), bf16)]
        + [dma((12,)), dma((3,)), dma((4,)), dma((3,)), dma((3,)), dma]
        + [dma((4,)), dma((2,)), dma((2,)), dma, dma],
        compiler_params=pltpu.CompilerParams(collective_id=0, has_side_effects=True),
    )(skip[None, :], norm_gain[None, :], routes.T, *far)
    return tuple(
        pl.pallas_call(
            publish_kernel,
            out_shape=(local, local),
            in_specs=[here] * 2,
            out_specs=(here, here),
        )(*results)
    )


def solution(mesh):
    in_specs = (
        P("ctx", "ch"),
        P("ctx", "ch"),
        P("ctx", "ch"),
        P("ch"),
        P(),
        P(),
        P("ctx", None, None),
        P("ctx", None, None),
        P(("ctx", "ch"), None),
    )
    out_specs = (P("ctx", "ch"), P("ctx", "ch"))
    return jax.shard_map(body, mesh=mesh, in_specs=in_specs, out_specs=out_specs, check_vma=False)
```

```python
import math

import jax
import jax.numpy as jnp
import numpy as np
from jax import lax
from jax.experimental import pallas as pl
from jax.experimental.pallas import tpu as pltpu
from jax.sharding import PartitionSpec as P

CAP = 16
bf16 = jnp.bfloat16
f32 = jnp.float32


def dft_constants(shards, tok, chans):
    total = shards * tok
    fields = 2 * chans
    row = np.arange(shards)
    col = np.arange(tok)
    outer = 2.0 * np.pi * row[None, :] * (row[:, None] + 0.25) / shards
    first = np.concatenate([np.cos(outer), -np.sin(outer)], axis=0)
    first = np.repeat(first, fields, axis=1)
    last = np.concatenate([np.cos(outer.T), -np.sin(outer.T)], axis=1) / total
    last = np.repeat(last, fields, axis=0)
    turn = 2.0 * np.pi * (row[:, None] + 0.25) * col[None, :] / total
    inner = 2.0 * np.pi * ((col[:, None] * col[None, :]) % tok) / tok
    as16 = lambda a: jnp.asarray(a.astype(np.float32), bf16)
    as32 = lambda a: jnp.asarray(a.astype(np.float32))
    return (
        as16(first),
        as32(np.cos(turn)),
        as32(-np.sin(turn)),
        as16(np.cos(inner)),
        as16(np.sin(inner)),
        as16(last),
    )


def dot(a, b):
    return jnp.dot(a, b, preferred_element_type=f32)


def iota(shape, axis):
    return lax.broadcasted_iota(jnp.int32, shape, axis)


def one_hot(mask):
    return mask.astype(f32).astype(bf16)


def contract(a, b, axis_a, axis_b):
    return lax.dot_general(a, b, (((axis_a,), (axis_b,)), ((), ())), preferred_element_type=f32)


def pack(signal, taps, shards, fields):
    chans = fields // 2
    shape = (shards * fields, signal.shape[1])
    row, chan = iota(shape, 0), iota(shape, 1)
    field = row % fields
    mine = row // fields * chans + field % chans == chan
    sig = contract(one_hot(mine & (field < chans)), signal, 1, 1)
    tap = contract(one_hot(mine & (field >= chans)), taps.astype(bf16), 1, 1)
    return sig + tap


def convolve(data, tables, re_ref, im_ref, shards, chans):
    first, tr, ti, cos, sin = (table[...] for table in tables[:5])
    fields = 2 * chans
    lane = iota(first.shape, 1) % fields
    for field in range(fields):
        g = dot(jnp.where(lane == field, first, jnp.zeros_like(first)), data)
        g_re, g_im = g[:shards], g[shards:]
        rows = pl.ds(field * shards, shards)
        re_ref[rows, :] = (g_re * tr - g_im * ti).astype(bf16)
        im_ref[rows, :] = (g_re * ti + g_im * tr).astype(bf16)
    re, im = re_ref[...], im_ref[...]
    x_re = dot(re, cos) + dot(im, sin)
    x_im = dot(im, cos) - dot(re, sin)
    half = chans * shards
    p_re = (x_re[:half] * x_re[half:] - x_im[:half] * x_im[half:]).astype(bf16)
    p_im = (x_re[:half] * x_im[half:] + x_im[:half] * x_re[half:]).astype(bf16)
    g_re = dot(p_re, cos) - dot(p_im, sin)
    g_im = dot(p_im, cos) + dot(p_re, sin)
    pairs = []
    for chan in range(chans):
        rows = slice(chan * shards, (chan + 1) * shards)
        a = (g_re[rows] * tr + g_im[rows] * ti).astype(bf16)
        b = (g_im[rows] * tr - g_re[rows] * ti).astype(bf16)
        pairs.append(jnp.concatenate([a, b], axis=0))
    return pairs


def last_step(pairs, last, side):
    chans = len(pairs)
    row = iota(last.shape, 0) % (2 * chans)
    count = pairs[0].shape[1] // 4
    total = jnp.zeros((last.shape[0], count), f32)
    for chan, pair in enumerate(pairs):
        for part in range(2):
            table = jnp.where(row == part * chans + chan, last, jnp.zeros_like(last))
            start = (2 * side + part) * count
            total += dot(table, pair[:, start : start + count])
    return total


def unpack(data, side, fields):
    chans = fields // 2
    shape = (data.shape[0], data.shape[0] // fields * chans)
    row, chan = iota(shape, 0), iota(shape, 1)
    field = row % fields
    mine = (row // fields * chans + field % chans == chan) & (field // chans == side)
    return contract(data, one_hot(mine), 0, 0)


def slots_of(routes_t, experts):
    count = routes_t.shape[1]
    slots = experts * CAP
    ids = iota((experts, count), 0)
    named = one_hot((routes_t[0:1, :] == ids) | (routes_t[1:2, :] == ids))
    rank = dot(named, one_hot(iota((count, count), 0) < iota((count, count), 1))).astype(bf16)
    spread = one_hot(iota((slots, experts), 0) // CAP == iota((slots, experts), 1))
    slot = (iota((slots, count), 0) % CAP).astype(f32)
    return one_hot((dot(spread, named) > 0.5) & (dot(spread, rank) == slot))


def normalize(x, gain):
    scale = lax.rsqrt(jnp.mean(x * x, axis=-1, keepdims=True) + 1e-05)
    return (x * scale * gain).astype(bf16)


def remote(src, dst, send_sem, recv_sem, **where):
    return pltpu.make_async_remote_copy(
        src_ref=src,
        dst_ref=dst,
        send_sem=send_sem,
        recv_sem=recv_sem,
        device_id=where,
        device_id_type=pl.DeviceIdType.MESH,
    )


class Place:
    def __init__(self, zs=8, xs=4):
        self.zs, self.xs = zs, xs
        self.me = lax.axis_index("ctx")
        self.y = lax.axis_index("ch")
        self.core = self.me % 2
        self.chip = self.me // 2
        self.z = self.chip // xs
        self.x = self.chip % xs
        self.twin = self.me + 1 - 2 * self.core

    def at(self, dz, dx):
        return (self.z + dz + self.zs) % self.zs * self.xs + (self.x + dx + self.xs) % self.xs


def greet(place, count, ys):
    barrier = pltpu.get_barrier_semaphore()

    def tell(**where):
        pl.semaphore_signal(barrier, inc=1, device_id=where, device_id_type=pl.DeviceIdType.MESH)

    def shard(i, carry):
        tell(ctx=(place.me + i) % count)
        return carry

    lax.fori_loop(1, count, shard, 0)
    for dy in range(1, ys):
        tell(ch=(place.y + dy) % ys)
    return lambda: pl.semaphore_wait(barrier, count - 1 + ys - 1)


def offsets(q, half, j):
    if half == 0:
        return 4 - q, j
    return (4 + q if q else 0), (j + 1) % 4


def each(q, act):
    for half in range(2):

        def one(j, carry):
            dz, dx = offsets(q, half, j)
            act(q * 8 + half * 4 + j, dz, dx)
            return carry

        lax.fori_loop(0, 3 if q == 0 and half == 1 else 4, one, 0)


def split(refs, counts):
    refs = list(refs)
    return [[refs.pop(0) for _ in range(count)] for count in counts]


def publish_kernel(a_ref, b_ref, a_out, b_out):
    a_out[...] = a_ref[...]
    b_out[...] = b_ref[...]


def layer_kernel(skip, gain, routes_t, *rest):
    place = Place()
    me, core, chip, y = place.me, place.core, place.chip, place.y
    (
        far, (mixed_out, out),
        near, (packed, fields, re_ref, im_ref, conv_out, conv_in, routes_all),
        (send, here, got, summed, back, ups, downs),
        (far_sem, local_sem, conv_sem, xs_sem, xr_sem, send_sem, got_sem, ws_sem, wr_sem, rs_sem, back_sem),
    ) = split(rest, (12, 2, 10, 7, 7, 11))
    shards, width_ch = 64, near[0].shape[1]
    chans = width_ch // shards
    chips, groups, chunk = 32, 4, 8
    ready = greet(place, shards, groups)
    near = (*near, ups.at[0], downs.at[0])
    fetches = [pltpu.make_async_copy(a, b, far_sem.at[i]) for i, (a, b) in enumerate(zip(far, near))]
    for fetch in fetches:
        fetch.start()
    signal, taps, gate, router_t, tables = near[0], near[1], near[2], near[3], near[4:10]
    fetches[0].wait()
    fetches[1].wait()
    packed[...] = pack(signal[...], taps[...], shards, 2 * chans).reshape(packed.shape).astype(bf16)
    routes_all[y] = routes_t[...]
    for fetch in fetches[2:]:
        fetch.wait()
    ready()

    def spread_out(source, target, ss, rs, stay_sem):
        def both(to):
            for side in range(2):
                where = to * 2 + side
                remote(source.at[where], target.at[me], ss, rs, ctx=where).start()

        for q in range(4):
            each(q, lambda slot, dz, dx: both(place.at(dz, dx)))
        remote(source.at[place.twin], target.at[me], ss, rs, ctx=place.twin).start()
        stay = pltpu.make_async_copy(source.at[me], target.at[me], stay_sem)
        stay.start()
        most = pl.ds(0, shards - 1)
        whole = remote(source.at[most], target.at[most], ss, rs, ctx=place.twin)

        def arrive():
            whole.wait_recv()
            stay.wait()

        return whole, arrive

    tells = [
        remote(routes_t, routes_all.at[y], xs_sem.at[dy - 1], xr_sem.at[dy - 1], ch=(y + dy) % groups)
        for dy in range(1, groups)
    ]

    def all_slots():
        for tell in tells:
            tell.wait()
        for k in range(groups):
            here[k] = slots_of(routes_all[k], chips)

    swaps = [
        remote(both.at[0], both.at[1], ws_sem.at[i], wr_sem.at[i], ctx=place.twin)
        for i, both in enumerate((ups, downs))
    ]
    for tell in tells:
        tell.start()
    whole, arrive = spread_out(packed, fields, conv_sem.at[0], conv_sem.at[1], local_sem.at[2])
    all_slots()
    arrive()
    for swap in swaps:
        swap.start()
    data = fields[...].astype(f32).reshape(shards * 2 * chans, -1).astype(bf16)
    pairs = convolve(data, tables, re_ref, im_ref, shards, chans)
    returns = []
    for side in range(2):
        conv_out[side] = last_step(pairs, tables[5][...], side).reshape(conv_out.shape[1:]).astype(bf16)
        returns.append(
            spread_out(
                conv_out.at[side], conv_in.at[side], conv_sem.at[2 + 2 * side], conv_sem.at[3 + 2 * side],
                local_sem.at[3 + side],
            )
        )
    mine = y * chips + chip
    keep = pltpu.make_async_copy(send.at[mine], got.at[y * chips + 7], local_sem.at[0])
    for side in range(2):
        returns[side][1]()
        data = conv_in[side].astype(f32).reshape(shards * 2 * chans, -1).astype(bf16)
        for part in range(2):
            k = 2 * side + part
            conv = unpack(data, part, 2 * chans)
            count = conv.shape[0]
            span = slice(k * count, (k + 1) * count)
            sig = signal[span, :].astype(f32)
            value = (gate[span, :].astype(f32) * (conv + skip[...] * sig)).astype(bf16)
            mixed_out[span, :] = value
            send[k * chips : (k + 1) * chips] = dot(here[k], value).astype(bf16).reshape(chips, CAP, width_ch)

        for q in range(4):

            def dispatch(slot, dz, dx):
                to = place.at(dz, dx)
                for k in range(2 * side, 2 * side + 2):
                    remote(
                        send.at[k * chips + to], got.at[y * chips + slot], send_sem, got_sem.at[q],
                        ctx=to * 2 + core, ch=k,
                    ).start()

            each(q, dispatch)
            for k in range(2 * side, 2 * side + 2) if q == 0 else ():

                @pl.when(y != k)
                def _():
                    remote(
                        send.at[k * chips + chip], got.at[y * chips + 7], send_sem, got_sem.at[0], ch=k
                    ).start()

                pl.when(y == k)(keep.start)

    keep_back = pltpu.make_async_copy(summed.at[y * chips + 7], back.at[mine], local_sem.at[1])
    whole.wait_send()
    for back_half, _ in returns:
        back_half.wait_send()
    for swap in swaps:
        swap.wait()
    column = router_t[pl.ds(chip, 1), :]
    for q in range(4):
        came = pl.ds(0, groups * chunk - (q == 0))
        remote(send.at[came], got.at[came], send_sem, got_sem.at[q], ctx=me).wait_recv()
        if q == 0:
            keep.wait()
        slices = [got[k * chips + q * chunk : k * chips + (q + 1) * chunk] for k in range(groups)]
        x = jnp.concatenate([piece.reshape(chunk * CAP, width_ch) for piece in slices], axis=1)
        normed = normalize(x.astype(f32), gain[...])
        logit = jnp.sum(normed.astype(f32) * column, axis=-1, keepdims=True)
        total = None
        for half in range(2):
            hidden = jax.nn.gelu(dot(normed, ups[half]), approximate=True).astype(bf16)
            part = dot(hidden, downs[half])
            total = part if half == 0 else total + part
        total = (jax.nn.sigmoid(logit) * total).astype(bf16)
        for k in range(groups):
            piece = total[:, k * width_ch : (k + 1) * width_ch].reshape(chunk, CAP, width_ch)
            summed[k * chips + q * chunk : k * chips + (q + 1) * chunk] = piece

        def give_back(slot, dz, dx):
            to = place.at(-dz, -dx) * 2 + core
            for k in range(groups):
                remote(
                    summed.at[k * chips + slot], back.at[mine], rs_sem, back_sem, ctx=to, ch=k
                ).start()

        each(q, give_back)
        if q == 0:
            for dy in range(1, groups):
                k = (y + dy) % groups
                remote(summed.at[k * chips + 7], back.at[mine], rs_sem, back_sem, ch=k).start()
            keep_back.start()
    keep_back.wait()
    others = pl.ds(0, groups * chips - 1)
    remote(summed.at[others], back.at[others], rs_sem, back_sem, ctx=me).wait_recv()
    for k in range(groups):
        slots = back[k * chips : (k + 1) * chips].reshape(chips * CAP, width_ch)
        rows = contract(here[k], slots, 0, 0).astype(bf16)
        out[k * rows.shape[0] : (k + 1) * rows.shape[0], :] = rows
    remote(send.at[others], got.at[others], send_sem, got_sem.at[0], ctx=me).wait_send()
    remote(summed.at[others], back.at[others], rs_sem, back_sem, ctx=me).wait_send()


def body(signal, gate_v, taps, skip, norm_gain, router, w_up, w_down, routes):
    tok_dev, ch_dev = signal.shape
    shards = lax.axis_size("ctx")
    groups = lax.axis_size("ch")
    chans = ch_dev // shards
    experts = router.shape[1]
    width = norm_gain.shape[0]
    rows = tok_dev // groups
    shape = jax.ShapeDtypeStruct
    far = (
        signal, taps, gate_v, router.T, *dft_constants(shards, tok_dev, chans), w_up[0], w_down[0],
    )
    hidden = w_up.shape[2]
    blocks = (groups * experts, CAP, ch_dev)
    dma = pltpu.SemaphoreType.DMA
    vmem = pltpu.VMEM
    here = pl.BlockSpec(memory_space=vmem)
    there = pl.BlockSpec(memory_space=pl.ANY)
    local = shape((tok_dev, ch_dev), bf16)
    results = pl.pallas_call(
        layer_kernel,
        out_shape=(local, local),
        in_specs=[here] * 3 + [there] * len(far),
        out_specs=(here, here),
        scratch_shapes=[vmem(a.shape, a.dtype) for a in far[:-2]]
        + [vmem((shards, 2 * chans, tok_dev), bf16)] * 2
        + [vmem((2 * chans * shards, tok_dev), bf16)] * 2
        + [vmem((2, shards, 2 * chans, tok_dev // 4), bf16)] * 2
        + [vmem((groups, 2, rows), routes.dtype)]
        + [vmem(blocks, bf16)]
        + [vmem((groups, experts * CAP, rows), bf16)]
        + [vmem(blocks, bf16)] * 3
        + [vmem((2, width, hidden), bf16), vmem((2, hidden, width), bf16)]
        + [dma((12,)), dma((5,)), dma((6,)), dma((3,)), dma((3,)), dma]
        + [dma((4,)), dma((2,)), dma((2,)), dma, dma],
        compiler_params=pltpu.CompilerParams(collective_id=0, has_side_effects=True),
    )(skip[None, :], norm_gain[None, :], routes.T, *far)
    return tuple(
        pl.pallas_call(
            publish_kernel,
            out_shape=(local, local),
            in_specs=[here] * 2,
            out_specs=(here, here),
        )(*results)
    )


def solution(mesh):
    in_specs = (
        P("ctx", "ch"),
        P("ctx", "ch"),
        P("ctx", "ch"),
        P("ch"),
        P(),
        P(),
        P("ctx", None, None),
        P("ctx", None, None),
        P(("ctx", "ch"), None),
    )
    out_specs = (P("ctx", "ch"), P("ctx", "ch"))
    return jax.shard_map(body, mesh=mesh, in_specs=in_specs, out_specs=out_specs, check_vma=False)
```

```python
import math

import jax
import jax.numpy as jnp
import numpy as np
from jax import lax
from jax.experimental import pallas as pl
from jax.experimental.pallas import tpu as pltpu
from jax.sharding import PartitionSpec as P

CAP = 16
bf16 = jnp.bfloat16
f32 = jnp.float32


def dft_constants(shards, tok, chans):
    total = shards * tok
    fields = 2 * chans
    row = np.arange(shards)
    col = np.arange(tok)
    outer = 2.0 * np.pi * row[None, :] * (row[:, None] + 0.25) / shards
    first = np.concatenate([np.cos(outer), -np.sin(outer)], axis=0)
    first = np.repeat(first, fields, axis=1)
    last = np.concatenate([np.cos(outer.T), -np.sin(outer.T)], axis=1) / total
    last = np.repeat(last, fields, axis=0)
    turn = 2.0 * np.pi * (row[:, None] + 0.25) * col[None, :] / total
    inner = 2.0 * np.pi * ((col[:, None] * col[None, :]) % tok) / tok
    as16 = lambda a: jnp.asarray(a.astype(np.float32), bf16)
    as32 = lambda a: jnp.asarray(a.astype(np.float32))
    return (
        as16(first),
        as32(np.cos(turn)),
        as32(-np.sin(turn)),
        as16(np.cos(inner)),
        as16(np.sin(inner)),
        as16(last),
    )


def dot(a, b):
    return jnp.dot(a, b, preferred_element_type=f32)


def iota(shape, axis):
    return lax.broadcasted_iota(jnp.int32, shape, axis)


def one_hot(mask):
    return mask.astype(f32).astype(bf16)


def contract(a, b, axis_a, axis_b):
    return lax.dot_general(a, b, (((axis_a,), (axis_b,)), ((), ())), preferred_element_type=f32)


def pack(signal, taps, shards, fields):
    chans = fields // 2
    shape = (shards * fields, signal.shape[1])
    row, chan = iota(shape, 0), iota(shape, 1)
    field = row % fields
    mine = row // fields * chans + field % chans == chan
    sig = contract(one_hot(mine & (field < chans)), signal, 1, 1)
    tap = contract(one_hot(mine & (field >= chans)), taps.astype(bf16), 1, 1)
    return sig + tap


def convolve(data, tables, re_ref, im_ref, shards, chans):
    first, tr, ti, cos, sin = (table[...] for table in tables[:5])
    fields = 2 * chans
    lane = iota(first.shape, 1) % fields
    for field in range(fields):
        g = dot(jnp.where(lane == field, first, jnp.zeros_like(first)), data)
        g_re, g_im = g[:shards], g[shards:]
        rows = pl.ds(field * shards, shards)
        re_ref[rows, :] = (g_re * tr - g_im * ti).astype(bf16)
        im_ref[rows, :] = (g_re * ti + g_im * tr).astype(bf16)
    re, im = re_ref[...], im_ref[...]
    x_re = dot(re, cos) + dot(im, sin)
    x_im = dot(im, cos) - dot(re, sin)
    half = chans * shards
    p_re = (x_re[:half] * x_re[half:] - x_im[:half] * x_im[half:]).astype(bf16)
    p_im = (x_re[:half] * x_im[half:] + x_im[:half] * x_re[half:]).astype(bf16)
    return p_re, p_im


def last_step(product, tables, side, shards, chans):
    p_re, p_im = product
    count = tables[1].shape[1] // 4
    span = pl.ds(2 * side * count, 2 * count)
    tr, ti, cos, sin = (table[:, span] for table in tables[1:5])
    last = tables[5][...]
    g_re = dot(p_re, cos) - dot(p_im, sin)
    g_im = dot(p_im, cos) + dot(p_re, sin)
    row = iota(last.shape, 0) % (2 * chans)
    total = jnp.zeros((last.shape[0], count), f32)
    for chan in range(chans):
        rows = slice(chan * shards, (chan + 1) * shards)
        a = (g_re[rows] * tr + g_im[rows] * ti).astype(bf16)
        b = (g_im[rows] * tr - g_re[rows] * ti).astype(bf16)
        pair = jnp.concatenate([a, b], axis=0)
        for part in range(2):
            table = jnp.where(row == part * chans + chan, last, jnp.zeros_like(last))
            total += dot(table, pair[:, part * count : (part + 1) * count])
    return total


def unpack(data, side, fields):
    chans = fields // 2
    shape = (data.shape[0], data.shape[0] // fields * chans)
    row, chan = iota(shape, 0), iota(shape, 1)
    field = row % fields
    mine = (row // fields * chans + field % chans == chan) & (field // chans == side)
    return contract(data, one_hot(mine), 0, 0)


def slots_of(routes_t, experts):
    count = routes_t.shape[1]
    slots = experts * CAP
    ids = iota((experts, count), 0)
    named = one_hot((routes_t[0:1, :] == ids) | (routes_t[1:2, :] == ids))
    rank = dot(named, one_hot(iota((count, count), 0) < iota((count, count), 1))).astype(bf16)
    spread = one_hot(iota((slots, experts), 0) // CAP == iota((slots, experts), 1))
    slot = (iota((slots, count), 0) % CAP).astype(f32)
    return one_hot((dot(spread, named) > 0.5) & (dot(spread, rank) == slot))


def normalize(x, gain):
    scale = lax.rsqrt(jnp.mean(x * x, axis=-1, keepdims=True) + 1e-05)
    return (x * scale * gain).astype(bf16)


def remote(src, dst, send_sem, recv_sem, **where):
    return pltpu.make_async_remote_copy(
        src_ref=src,
        dst_ref=dst,
        send_sem=send_sem,
        recv_sem=recv_sem,
        device_id=where,
        device_id_type=pl.DeviceIdType.MESH,
    )


class Place:
    def __init__(self, zs=8, xs=4):
        self.zs, self.xs = zs, xs
        self.me = lax.axis_index("ctx")
        self.y = lax.axis_index("ch")
        self.core = self.me % 2
        self.chip = self.me // 2
        self.z = self.chip // xs
        self.x = self.chip % xs
        self.twin = self.me + 1 - 2 * self.core

    def at(self, dz, dx):
        return (self.z + dz + self.zs) % self.zs * self.xs + (self.x + dx + self.xs) % self.xs


def greet(place, count, ys):
    barrier = pltpu.get_barrier_semaphore()

    def tell(**where):
        pl.semaphore_signal(barrier, inc=1, device_id=where, device_id_type=pl.DeviceIdType.MESH)

    tell(ctx=(place.me + count // 2) % count)

    def shard(i, carry):
        tell(ctx=(place.me + count // 2 + i) % count)
        tell(ctx=(place.me + count // 2 - i) % count)
        return carry

    lax.fori_loop(1, count // 2, shard, 0)
    for dy in range(1, ys):
        tell(ch=(place.y + dy) % ys)
    return lambda: pl.semaphore_wait(barrier, count - 1 + ys - 1)


def offsets(q, half, j):
    if half == 0:
        return 4 - q, j
    return (4 + q if q else 0), (j + 1) % 4


def each(q, act):
    for half in range(2):

        def one(j, carry):
            dz, dx = offsets(q, half, j)
            act(q * 8 + half * 4 + j, dz, dx)
            return carry

        lax.fori_loop(0, 3 if q == 0 and half == 1 else 4, one, 0)


def split(refs, counts):
    refs = list(refs)
    return [[refs.pop(0) for _ in range(count)] for count in counts]


def publish_kernel(a_ref, b_ref, a_out, b_out):
    a_out[...] = a_ref[...]
    b_out[...] = b_ref[...]


def layer_kernel(skip, gain, routes_t, *rest):
    place = Place()
    me, core, chip, y = place.me, place.core, place.chip, place.y
    (
        far, (mixed_out, out),
        near, (packed, fields, re_ref, im_ref, conv_out, conv_in, routes_all),
        (send, here, turned, got, summed, back, ups, downs),
        (far_sem, local_sem, conv_sem, xs_sem, xr_sem, send_sem, got_sem, ws_sem, wr_sem, rs_sem, back_sem),
    ) = split(rest, (12, 2, 10, 7, 8, 11))
    shards, width_ch = 64, near[0].shape[1]
    chans = width_ch // shards
    chips, groups, chunk = 32, 4, 8
    ready = greet(place, shards, groups)
    near = (*near, ups.at[0], downs.at[0])
    fetches = [pltpu.make_async_copy(a, b, far_sem.at[i]) for i, (a, b) in enumerate(zip(far, near))]
    for fetch in fetches:
        fetch.start()
    signal, taps, gate, router_t, tables = near[0], near[1], near[2], near[3], near[4:10]
    fetches[0].wait()
    fetches[1].wait()
    packed[...] = pack(signal[...], taps[...], shards, 2 * chans).reshape(packed.shape).astype(bf16)
    routes_all[y] = routes_t[...]
    for fetch in fetches[2:]:
        fetch.wait()
    ready()

    def spread_out(source, target, ss, rs, stay_sem):
        def both(to):
            for side in range(2):
                where = to * 2 + side
                remote(source.at[where], target.at[me], ss, rs, ctx=where).start()

        for q in range(4):
            each(q, lambda slot, dz, dx: both(place.at(dz, dx)))
        remote(source.at[place.twin], target.at[me], ss, rs, ctx=place.twin).start()
        stay = pltpu.make_async_copy(source.at[me], target.at[me], stay_sem)
        stay.start()
        most = pl.ds(0, shards - 1)
        whole = remote(source.at[most], target.at[most], ss, rs, ctx=place.twin)

        def arrive():
            whole.wait_recv()
            stay.wait()

        return whole, arrive

    tells = [
        remote(routes_t, routes_all.at[y], xs_sem.at[dy - 1], xr_sem.at[dy - 1], ch=(y + dy) % groups)
        for dy in range(1, groups)
    ]

    def all_slots():
        for tell in tells:
            tell.wait()
        for k in range(groups):
            here[k] = slots_of(routes_all[k], chips)

    swaps = [
        remote(both.at[0], both.at[1], ws_sem.at[i], wr_sem.at[i], ctx=place.twin)
        for i, both in enumerate((ups, downs))
    ]
    for tell in tells:
        tell.start()
    whole, arrive = spread_out(packed, fields, conv_sem.at[0], conv_sem.at[1], local_sem.at[2])
    all_slots()
    arrive()
    for swap in swaps:
        swap.start()
    data = fields[...].astype(f32).reshape(shards * 2 * chans, -1).astype(bf16)
    product = convolve(data, tables, re_ref, im_ref, shards, chans)
    returns = []
    for side in range(2):
        total = last_step(product, tables, side, shards, chans)
        conv_out[side] = total.reshape(conv_out.shape[1:]).astype(bf16)
        returns.append(
            spread_out(
                conv_out.at[side], conv_in.at[side], conv_sem.at[2 + 2 * side], conv_sem.at[3 + 2 * side],
                local_sem.at[3 + side],
            )
        )
    mine = y * chips + chip
    keep = pltpu.make_async_copy(send.at[mine], got.at[y * chips + 7], local_sem.at[0])
    for side in range(2):
        returns[side][1]()
        data = conv_in[side].astype(f32).reshape(shards * 2 * chans, -1).astype(bf16)
        for part in range(2):
            k = 2 * side + part
            conv = unpack(data, part, 2 * chans)
            count = conv.shape[0]
            span = slice(k * count, (k + 1) * count)
            sig = signal[span, :].astype(f32)
            value = (gate[span, :].astype(f32) * (conv + skip[...] * sig)).astype(bf16)
            mixed_out[span, :] = value
            send[k * chips : (k + 1) * chips] = dot(here[k], value).astype(bf16).reshape(chips, CAP, width_ch)

        for q in range(4):

            def dispatch(slot, dz, dx):
                to = place.at(dz, dx)
                for k in range(2 * side, 2 * side + 2):
                    remote(
                        send.at[k * chips + to], got.at[y * chips + slot], send_sem, got_sem.at[q],
                        ctx=to * 2 + core, ch=k,
                    ).start()

            each(q, dispatch)
            for k in range(2 * side, 2 * side + 2) if q == 0 else ():

                @pl.when(y != k)
                def _():
                    remote(
                        send.at[k * chips + chip], got.at[y * chips + 7], send_sem, got_sem.at[0], ch=k
                    ).start()

                pl.when(y == k)(keep.start)

    keep_back = pltpu.make_async_copy(summed.at[y * chips + 7], back.at[mine], local_sem.at[1])
    whole.wait_send()
    for back_half, _ in returns:
        back_half.wait_send()
    for swap in swaps:
        swap.wait()
    column = router_t[pl.ds(chip, 1), :]
    count = here.shape[2]
    turn = one_hot(iota((count, count), 0) == iota((count, count), 1))
    for k in range(groups):
        turned[k] = contract(turn, here[k], 1, 1).astype(bf16)
    for q in range(4):
        came = pl.ds(0, groups * chunk - (q == 0))
        remote(send.at[came], got.at[came], send_sem, got_sem.at[q], ctx=me).wait_recv()
        if q == 0:
            keep.wait()
        slices = [got[k * chips + q * chunk : k * chips + (q + 1) * chunk] for k in range(groups)]
        x = jnp.concatenate([piece.reshape(chunk * CAP, width_ch) for piece in slices], axis=1)
        normed = normalize(x.astype(f32), gain[...])
        logit = jnp.sum(normed.astype(f32) * column, axis=-1, keepdims=True)
        total = None
        for half in range(2):
            hidden = jax.nn.gelu(dot(normed, ups[half]), approximate=True).astype(bf16)
            part = dot(hidden, downs[half])
            total = part if half == 0 else total + part
        total = (jax.nn.sigmoid(logit) * total).astype(bf16)
        for k in range(groups):
            piece = total[:, k * width_ch : (k + 1) * width_ch].reshape(chunk, CAP, width_ch)
            summed[k * chips + q * chunk : k * chips + (q + 1) * chunk] = piece

        def give_back(slot, dz, dx):
            to = place.at(-dz, -dx) * 2 + core
            for k in range(groups):
                remote(
                    summed.at[k * chips + slot], back.at[mine], rs_sem, back_sem, ctx=to, ch=k
                ).start()

        each(q, give_back)
        if q == 0:
            for dy in range(1, groups):
                k = (y + dy) % groups
                remote(summed.at[k * chips + 7], back.at[mine], rs_sem, back_sem, ch=k).start()
            keep_back.start()
    keep_back.wait()
    others = pl.ds(0, groups * chips - 1)
    remote(summed.at[others], back.at[others], rs_sem, back_sem, ctx=me).wait_recv()
    for k in range(groups):
        slots = back[k * chips : (k + 1) * chips].reshape(chips * CAP, width_ch)
        rows = dot(turned[k], slots).astype(bf16)
        out[k * rows.shape[0] : (k + 1) * rows.shape[0], :] = rows
    remote(send.at[others], got.at[others], send_sem, got_sem.at[0], ctx=me).wait_send()
    remote(summed.at[others], back.at[others], rs_sem, back_sem, ctx=me).wait_send()


def body(signal, gate_v, taps, skip, norm_gain, router, w_up, w_down, routes):
    tok_dev, ch_dev = signal.shape
    shards = lax.axis_size("ctx")
    groups = lax.axis_size("ch")
    chans = ch_dev // shards
    experts = router.shape[1]
    width = norm_gain.shape[0]
    rows = tok_dev // groups
    shape = jax.ShapeDtypeStruct
    far = (
        signal, taps, gate_v, router.T, *dft_constants(shards, tok_dev, chans), w_up[0], w_down[0],
    )
    hidden = w_up.shape[2]
    blocks = (groups * experts, CAP, ch_dev)
    dma = pltpu.SemaphoreType.DMA
    vmem = pltpu.VMEM
    here = pl.BlockSpec(memory_space=vmem)
    there = pl.BlockSpec(memory_space=pl.ANY)
    local = shape((tok_dev, ch_dev), bf16)
    results = pl.pallas_call(
        layer_kernel,
        out_shape=(local, local),
        in_specs=[here] * 3 + [there] * len(far),
        out_specs=(here, here),
        scratch_shapes=[vmem(a.shape, a.dtype) for a in far[:-2]]
        + [vmem((shards, 2 * chans, tok_dev), bf16)] * 2
        + [vmem((2 * chans * shards, tok_dev), bf16)] * 2
        + [vmem((2, shards, 2 * chans, tok_dev // 4), bf16)] * 2
        + [vmem((groups, 2, rows), routes.dtype)]
        + [vmem(blocks, bf16)]
        + [vmem((groups, experts * CAP, rows), bf16), vmem((groups, rows, experts * CAP), bf16)]
        + [vmem(blocks, bf16)] * 3
        + [vmem((2, width, hidden), bf16), vmem((2, hidden, width), bf16)]
        + [dma((12,)), dma((5,)), dma((6,)), dma((3,)), dma((3,)), dma]
        + [dma((4,)), dma((2,)), dma((2,)), dma, dma],
        compiler_params=pltpu.CompilerParams(collective_id=0, has_side_effects=True),
    )(skip[None, :], norm_gain[None, :], routes.T, *far)
    return tuple(
        pl.pallas_call(
            publish_kernel,
            out_shape=(local, local),
            in_specs=[here] * 2,
            out_specs=(here, here),
        )(*results)
    )


def solution(mesh):
    in_specs = (
        P("ctx", "ch"),
        P("ctx", "ch"),
        P("ctx", "ch"),
        P("ch"),
        P(),
        P(),
        P("ctx", None, None),
        P("ctx", None, None),
        P(("ctx", "ch"), None),
    )
    out_specs = (P("ctx", "ch"), P("ctx", "ch"))
    return jax.shard_map(body, mesh=mesh, in_specs=in_specs, out_specs=out_specs, check_vma=False)
```

```python
import math

import jax
import jax.numpy as jnp
import numpy as np
from jax import lax
from jax.experimental import pallas as pl
from jax.experimental.pallas import tpu as pltpu
from jax.sharding import PartitionSpec as P

CAP = 16
bf16 = jnp.bfloat16
f32 = jnp.float32


def dft_constants(shards, tok, chans):
    total = shards * tok
    fields = 2 * chans
    row = np.arange(shards)
    col = np.arange(tok)
    outer = 2.0 * np.pi * row[None, :] * (row[:, None] + 0.25) / shards
    first = np.concatenate([np.cos(outer), -np.sin(outer)], axis=0)
    first = np.repeat(first, fields, axis=1)
    last = np.concatenate([np.cos(outer.T), -np.sin(outer.T)], axis=1) / total
    last = np.repeat(last, fields, axis=0)
    turn = 2.0 * np.pi * (row[:, None] + 0.25) * col[None, :] / total
    inner = 2.0 * np.pi * ((col[:, None] * col[None, :]) % tok) / tok
    as16 = lambda a: jnp.asarray(a.astype(np.float32), bf16)
    as32 = lambda a: jnp.asarray(a.astype(np.float32))
    return (
        as16(first),
        as32(np.cos(turn)),
        as32(-np.sin(turn)),
        as16(np.cos(inner)),
        as16(np.sin(inner)),
        as16(last),
    )


def dot(a, b):
    return jnp.dot(a, b, preferred_element_type=f32)


def iota(shape, axis):
    return lax.broadcasted_iota(jnp.int32, shape, axis)


def one_hot(mask):
    return mask.astype(f32).astype(bf16)


def contract(a, b, axis_a, axis_b):
    return lax.dot_general(a, b, (((axis_a,), (axis_b,)), ((), ())), preferred_element_type=f32)


def pack(signal, taps, shards, fields):
    chans = fields // 2
    shape = (shards * fields, signal.shape[1])
    row, chan = iota(shape, 0), iota(shape, 1)
    field = row % fields
    mine = row // fields * chans + field % chans == chan
    sig = contract(one_hot(mine & (field < chans)), signal, 1, 1)
    tap = contract(one_hot(mine & (field >= chans)), taps.astype(bf16), 1, 1)
    return sig + tap


def convolve(data, tables, re_ref, im_ref, shards, chans):
    first, tr, ti, cos, sin = (table[...] for table in tables[:5])
    fields = 2 * chans
    lane = iota(first.shape, 1) % fields
    for field in range(fields):
        g = dot(jnp.where(lane == field, first, jnp.zeros_like(first)), data)
        g_re, g_im = g[:shards], g[shards:]
        rows = pl.ds(field * shards, shards)
        re_ref[rows, :] = (g_re * tr - g_im * ti).astype(bf16)
        im_ref[rows, :] = (g_re * ti + g_im * tr).astype(bf16)
    re, im = re_ref[...], im_ref[...]
    x_re = dot(re, cos) + dot(im, sin)
    x_im = dot(im, cos) - dot(re, sin)
    half = chans * shards
    p_re = (x_re[:half] * x_re[half:] - x_im[:half] * x_im[half:]).astype(bf16)
    p_im = (x_re[:half] * x_im[half:] + x_im[:half] * x_re[half:]).astype(bf16)
    return p_re, p_im


def last_step(product, tables, side, shards, chans):
    p_re, p_im = product
    count = tables[1].shape[1] // 4
    span = pl.ds(2 * side * count, 2 * count)
    tr, ti, cos, sin = (table[:, span] for table in tables[1:5])
    last = tables[5][...]
    g_re = dot(p_re, cos) - dot(p_im, sin)
    g_im = dot(p_im, cos) + dot(p_re, sin)
    row = iota(last.shape, 0) % (2 * chans)
    total = jnp.zeros((last.shape[0], count), f32)
    for chan in range(chans):
        rows = slice(chan * shards, (chan + 1) * shards)
        a = (g_re[rows] * tr + g_im[rows] * ti).astype(bf16)
        b = (g_im[rows] * tr - g_re[rows] * ti).astype(bf16)
        pair = jnp.concatenate([a, b], axis=0)
        for part in range(2):
            table = jnp.where(row == part * chans + chan, last, jnp.zeros_like(last))
            total += dot(table, pair[:, part * count : (part + 1) * count])
    return total


def unpack(data, side, fields):
    chans = fields // 2
    shape = (data.shape[0], data.shape[0] // fields * chans)
    row, chan = iota(shape, 0), iota(shape, 1)
    field = row % fields
    mine = (row // fields * chans + field % chans == chan) & (field // chans == side)
    return contract(data, one_hot(mine), 0, 0)


def slots_of(routes_t, experts):
    count = routes_t.shape[1]
    slots = experts * CAP
    ids = iota((experts, count), 0)
    named = one_hot((routes_t[0:1, :] == ids) | (routes_t[1:2, :] == ids))
    rank = dot(named, one_hot(iota((count, count), 0) < iota((count, count), 1))).astype(bf16)
    spread = one_hot(iota((slots, experts), 0) // CAP == iota((slots, experts), 1))
    slot = (iota((slots, count), 0) % CAP).astype(f32)
    return one_hot((dot(spread, named) > 0.5) & (dot(spread, rank) == slot))


def normalize(x, gain):
    scale = lax.rsqrt(jnp.mean(x * x, axis=-1, keepdims=True) + 1e-05)
    return (x * scale * gain).astype(bf16)


def remote(src, dst, send_sem, recv_sem, **where):
    return pltpu.make_async_remote_copy(
        src_ref=src,
        dst_ref=dst,
        send_sem=send_sem,
        recv_sem=recv_sem,
        device_id=where,
        device_id_type=pl.DeviceIdType.MESH,
    )


class Place:
    def __init__(self, zs=8, xs=4):
        self.zs, self.xs = zs, xs
        self.me = lax.axis_index("ctx")
        self.y = lax.axis_index("ch")
        self.core = self.me % 2
        self.chip = self.me // 2
        self.z = self.chip // xs
        self.x = self.chip % xs
        self.twin = self.me + 1 - 2 * self.core

    def at(self, dz, dx):
        return (self.z + dz + self.zs) % self.zs * self.xs + (self.x + dx + self.xs) % self.xs


def greet(place, count, ys):
    barrier = pltpu.get_barrier_semaphore()

    def tell(**where):
        pl.semaphore_signal(barrier, inc=1, device_id=where, device_id_type=pl.DeviceIdType.MESH)

    tell(ctx=(place.me + count // 2) % count)

    def shard(i, carry):
        tell(ctx=(place.me + count // 2 + i) % count)
        tell(ctx=(place.me + count // 2 - i) % count)
        return carry

    lax.fori_loop(1, count // 2, shard, 0)
    for dy in range(1, ys):
        tell(ch=(place.y + dy) % ys)
    return lambda: pl.semaphore_wait(barrier, count - 1 + ys - 1)


def offsets(q, half, j):
    if half == 0:
        return 4 - q, j
    return (4 + q if q else 0), (j + 1) % 4


def each(q, act):
    for half in range(2):

        def one(j, carry):
            dz, dx = offsets(q, half, j)
            act(q * 8 + half * 4 + j, dz, dx)
            return carry

        lax.fori_loop(0, 3 if q == 0 and half == 1 else 4, one, 0)


def split(refs, counts):
    refs = list(refs)
    return [[refs.pop(0) for _ in range(count)] for count in counts]


def publish_kernel(a_ref, b_ref, a_out, b_out):
    a_out[...] = a_ref[...]
    b_out[...] = b_ref[...]


def layer_kernel(skip, gain, routes_t, *rest):
    place = Place()
    me, core, chip, y = place.me, place.core, place.chip, place.y
    (
        far, (mixed_out, out),
        near, (packed, fields, re_ref, im_ref, conv_out, conv_in, routes_all),
        (send, here, turned, got, summed, back, ups, downs),
        (far_sem, local_sem, conv_sem, xs_sem, xr_sem, send_sem, got_sem, ws_sem, wr_sem, rs_sem, back_sem),
    ) = split(rest, (12, 2, 10, 7, 8, 11))
    shards, width_ch = 64, near[0].shape[1]
    chans = width_ch // shards
    chips, groups, chunk = 32, 4, 8
    ready = greet(place, shards, groups)
    near = (*near, ups.at[0], downs.at[0])
    fetches = [pltpu.make_async_copy(a, b, far_sem.at[i]) for i, (a, b) in enumerate(zip(far, near))]
    for fetch in fetches:
        fetch.start()
    signal, taps, gate, router_t, tables = near[0], near[1], near[2], near[3], near[4:10]
    fetches[0].wait()
    fetches[1].wait()
    packed[...] = pack(signal[...], taps[...], shards, 2 * chans).reshape(packed.shape).astype(bf16)
    routes_all[y] = routes_t[...]
    for fetch in fetches[2:]:
        fetch.wait()
    ready()

    def spread_out(source, target, ss, rs, stay_sem):
        def both(to):
            for side in range(2):
                where = to * 2 + side
                remote(source.at[where], target.at[me], ss, rs, ctx=where).start()

        for q in range(4):
            each(q, lambda slot, dz, dx: both(place.at(dz, dx)))
        remote(source.at[place.twin], target.at[me], ss, rs, ctx=place.twin).start()
        stay = pltpu.make_async_copy(source.at[me], target.at[me], stay_sem)
        stay.start()
        most = pl.ds(0, shards - 1)
        whole = remote(source.at[most], target.at[most], ss, rs, ctx=place.twin)

        def arrive():
            whole.wait_recv()
            stay.wait()

        return whole, arrive

    tells = [
        remote(routes_t, routes_all.at[y], xs_sem.at[dy - 1], xr_sem.at[dy - 1], ch=(y + dy) % groups)
        for dy in range(1, groups)
    ]

    def all_slots():
        for tell in tells:
            tell.wait()
        for k in range(groups):
            here[k] = slots_of(routes_all[k], chips)

    swaps = [
        remote(both.at[0], both.at[1], ws_sem.at[i], wr_sem.at[i], ctx=place.twin)
        for i, both in enumerate((ups, downs))
    ]
    for tell in tells:
        tell.start()
    whole, arrive = spread_out(packed, fields, conv_sem.at[0], conv_sem.at[1], local_sem.at[2])
    all_slots()
    arrive()
    for swap in swaps:
        swap.start()
    data = fields[...].astype(f32).reshape(shards * 2 * chans, -1).astype(bf16)
    product = convolve(data, tables, re_ref, im_ref, shards, chans)
    returns = []
    for side in range(2):
        total = last_step(product, tables, side, shards, chans)
        conv_out[side] = total.reshape(conv_out.shape[1:]).astype(bf16)
        returns.append(
            spread_out(
                conv_out.at[side], conv_in.at[side], conv_sem.at[2 + 2 * side], conv_sem.at[3 + 2 * side],
                local_sem.at[3 + side],
            )
        )
    mine = y * chips + chip
    keep = pltpu.make_async_copy(send.at[mine], got.at[y * chips + 7], local_sem.at[0])
    for side in range(2):
        returns[side][1]()
        data = conv_in[side].astype(f32).reshape(shards * 2 * chans, -1).astype(bf16)
        for part in range(2):
            k = 2 * side + part
            conv = unpack(data, part, 2 * chans)
            count = conv.shape[0]
            span = slice(k * count, (k + 1) * count)
            sig = signal[span, :].astype(f32)
            value = (gate[span, :].astype(f32) * (conv + skip[...] * sig)).astype(bf16)
            mixed_out[span, :] = value
            send[k * chips : (k + 1) * chips] = dot(here[k], value).astype(bf16).reshape(chips, CAP, width_ch)

        for q in (0, 3, 2, 1):

            def dispatch(slot, dz, dx):
                to = place.at(dz, dx)
                for k in range(2 * side, 2 * side + 2):
                    remote(
                        send.at[k * chips + to], got.at[y * chips + slot], send_sem, got_sem.at[q],
                        ctx=to * 2 + core, ch=k,
                    ).start()

            each(q, dispatch)
            for k in range(2 * side, 2 * side + 2) if q == 0 else ():

                @pl.when(y != k)
                def _():
                    remote(
                        send.at[k * chips + chip], got.at[y * chips + 7], send_sem, got_sem.at[0], ch=k
                    ).start()

                pl.when(y == k)(keep.start)

    keep_back = pltpu.make_async_copy(summed.at[y * chips + 7], back.at[mine], local_sem.at[1])
    whole.wait_send()
    for back_half, _ in returns:
        back_half.wait_send()
    for swap in swaps:
        swap.wait()
    column = router_t[pl.ds(chip, 1), :]
    count = here.shape[2]
    turn = one_hot(iota((count, count), 0) == iota((count, count), 1))
    for k in range(groups):
        turned[k] = contract(turn, here[k], 1, 1).astype(bf16)
    for q in (0, 3, 2, 1):
        came = pl.ds(0, groups * chunk - (q == 0))
        remote(send.at[came], got.at[came], send_sem, got_sem.at[q], ctx=me).wait_recv()
        if q == 0:
            keep.wait()
        slices = [got[k * chips + q * chunk : k * chips + (q + 1) * chunk] for k in range(groups)]
        x = jnp.concatenate([piece.reshape(chunk * CAP, width_ch) for piece in slices], axis=1)
        normed = normalize(x.astype(f32), gain[...])
        logit = jnp.sum(normed.astype(f32) * column, axis=-1, keepdims=True)
        total = None
        for half in range(2):
            hidden = jax.nn.gelu(dot(normed, ups[half]), approximate=True).astype(bf16)
            part = dot(hidden, downs[half])
            total = part if half == 0 else total + part
        total = (jax.nn.sigmoid(logit) * total).astype(bf16)
        for k in range(groups):
            piece = total[:, k * width_ch : (k + 1) * width_ch].reshape(chunk, CAP, width_ch)
            summed[k * chips + q * chunk : k * chips + (q + 1) * chunk] = piece

        def give_back(slot, dz, dx):
            to = place.at(-dz, -dx) * 2 + core
            for k in range(groups):
                remote(
                    summed.at[k * chips + slot], back.at[mine], rs_sem, back_sem, ctx=to, ch=k
                ).start()

        each(q, give_back)
        if q == 0:
            for dy in range(1, groups):
                k = (y + dy) % groups
                remote(summed.at[k * chips + 7], back.at[mine], rs_sem, back_sem, ch=k).start()
            keep_back.start()
    keep_back.wait()
    others = pl.ds(0, groups * chips - 1)
    remote(summed.at[others], back.at[others], rs_sem, back_sem, ctx=me).wait_recv()
    for k in range(groups):
        slots = back[k * chips : (k + 1) * chips].reshape(chips * CAP, width_ch)
        rows = dot(turned[k], slots).astype(bf16)
        out[k * rows.shape[0] : (k + 1) * rows.shape[0], :] = rows
    remote(send.at[others], got.at[others], send_sem, got_sem.at[0], ctx=me).wait_send()
    remote(summed.at[others], back.at[others], rs_sem, back_sem, ctx=me).wait_send()


def body(signal, gate_v, taps, skip, norm_gain, router, w_up, w_down, routes):
    tok_dev, ch_dev = signal.shape
    shards = lax.axis_size("ctx")
    groups = lax.axis_size("ch")
    chans = ch_dev // shards
    experts = router.shape[1]
    width = norm_gain.shape[0]
    rows = tok_dev // groups
    shape = jax.ShapeDtypeStruct
    far = (
        signal, taps, gate_v, router.T, *dft_constants(shards, tok_dev, chans), w_up[0], w_down[0],
    )
    hidden = w_up.shape[2]
    blocks = (groups * experts, CAP, ch_dev)
    dma = pltpu.SemaphoreType.DMA
    vmem = pltpu.VMEM
    here = pl.BlockSpec(memory_space=vmem)
    there = pl.BlockSpec(memory_space=pl.ANY)
    local = shape((tok_dev, ch_dev), bf16)
    results = pl.pallas_call(
        layer_kernel,
        out_shape=(local, local),
        in_specs=[here] * 3 + [there] * len(far),
        out_specs=(here, here),
        scratch_shapes=[vmem(a.shape, a.dtype) for a in far[:-2]]
        + [vmem((shards, 2 * chans, tok_dev), bf16)] * 2
        + [vmem((2 * chans * shards, tok_dev), bf16)] * 2
        + [vmem((2, shards, 2 * chans, tok_dev // 4), bf16)] * 2
        + [vmem((groups, 2, rows), routes.dtype)]
        + [vmem(blocks, bf16)]
        + [vmem((groups, experts * CAP, rows), bf16), vmem((groups, rows, experts * CAP), bf16)]
        + [vmem(blocks, bf16)] * 3
        + [vmem((2, width, hidden), bf16), vmem((2, hidden, width), bf16)]
        + [dma((12,)), dma((5,)), dma((6,)), dma((3,)), dma((3,)), dma]
        + [dma((4,)), dma((2,)), dma((2,)), dma, dma],
        compiler_params=pltpu.CompilerParams(collective_id=0, has_side_effects=True),
    )(skip[None, :], norm_gain[None, :], routes.T, *far)
    return tuple(
        pl.pallas_call(
            publish_kernel,
            out_shape=(local, local),
            in_specs=[here] * 2,
            out_specs=(here, here),
        )(*results)
    )


def solution(mesh):
    in_specs = (
        P("ctx", "ch"),
        P("ctx", "ch"),
        P("ctx", "ch"),
        P("ch"),
        P(),
        P(),
        P("ctx", None, None),
        P("ctx", None, None),
        P(("ctx", "ch"), None),
    )
    out_specs = (P("ctx", "ch"), P("ctx", "ch"))
    return jax.shard_map(body, mesh=mesh, in_specs=in_specs, out_specs=out_specs, check_vma=False)
```

```python
import math

import jax
import jax.numpy as jnp
import numpy as np
from jax import lax
from jax.experimental import pallas as pl
from jax.experimental.pallas import tpu as pltpu
from jax.sharding import PartitionSpec as P

CAP = 16
bf16 = jnp.bfloat16
f32 = jnp.float32


def dft_constants(shards, tok, chans):
    total = shards * tok
    fields = 2 * chans
    row = np.arange(shards)
    col = np.arange(tok)
    outer = 2.0 * np.pi * row[None, :] * (row[:, None] + 0.25) / shards
    first = np.concatenate([np.cos(outer), -np.sin(outer)], axis=0)
    first = np.repeat(first, fields, axis=1)
    last = np.concatenate([np.cos(outer.T), -np.sin(outer.T)], axis=1) / total
    last = np.repeat(last, fields, axis=0)
    turn = 2.0 * np.pi * (row[:, None] + 0.25) * col[None, :] / total
    inner = 2.0 * np.pi * ((col[:, None] * col[None, :]) % tok) / tok
    as16 = lambda a: jnp.asarray(a.astype(np.float32), bf16)
    as32 = lambda a: jnp.asarray(a.astype(np.float32))
    return (
        as16(first),
        as32(np.cos(turn)),
        as32(-np.sin(turn)),
        as16(np.cos(inner)),
        as16(np.sin(inner)),
        as16(last),
    )


def dot(a, b):
    return jnp.dot(a, b, preferred_element_type=f32)


def iota(shape, axis):
    return lax.broadcasted_iota(jnp.int32, shape, axis)


def one_hot(mask):
    return mask.astype(f32).astype(bf16)


def contract(a, b, axis_a, axis_b):
    return lax.dot_general(a, b, (((axis_a,), (axis_b,)), ((), ())), preferred_element_type=f32)


def pack(signal, taps, shards, fields):
    chans = fields // 2
    shape = (shards * fields, signal.shape[1])
    row, chan = iota(shape, 0), iota(shape, 1)
    field = row % fields
    mine = row // fields * chans + field % chans == chan
    sig = contract(one_hot(mine & (field < chans)), signal, 1, 1)
    tap = contract(one_hot(mine & (field >= chans)), taps.astype(bf16), 1, 1)
    return sig + tap


def convolve(data, tables, re_ref, im_ref, shards, chans):
    first, tr, ti, cos, sin = (table[...] for table in tables[:5])
    fields = 2 * chans
    lane = iota(first.shape, 1) % fields
    for field in range(fields):
        g = dot(jnp.where(lane == field, first, jnp.zeros_like(first)), data)
        g_re, g_im = g[:shards], g[shards:]
        rows = pl.ds(field * shards, shards)
        re_ref[rows, :] = (g_re * tr - g_im * ti).astype(bf16)
        im_ref[rows, :] = (g_re * ti + g_im * tr).astype(bf16)
    re, im = re_ref[...], im_ref[...]
    x_re = dot(re, cos) + dot(im, sin)
    x_im = dot(im, cos) - dot(re, sin)
    half = chans * shards
    p_re = (x_re[:half] * x_re[half:] - x_im[:half] * x_im[half:]).astype(bf16)
    p_im = (x_re[:half] * x_im[half:] + x_im[:half] * x_re[half:]).astype(bf16)
    return p_re, p_im


def last_step(product, tables, side, shards, chans):
    p_re, p_im = product
    count = tables[1].shape[1] // 4
    span = pl.ds(2 * side * count, 2 * count)
    tr, ti, cos, sin = (table[:, span] for table in tables[1:5])
    last = tables[5][...]
    g_re = dot(p_re, cos) - dot(p_im, sin)
    g_im = dot(p_im, cos) + dot(p_re, sin)
    row = iota(last.shape, 0) % (2 * chans)
    total = jnp.zeros((last.shape[0], count), f32)
    for chan in range(chans):
        rows = slice(chan * shards, (chan + 1) * shards)
        a = (g_re[rows] * tr + g_im[rows] * ti).astype(bf16)
        b = (g_im[rows] * tr - g_re[rows] * ti).astype(bf16)
        pair = jnp.concatenate([a, b], axis=0)
        for part in range(2):
            table = jnp.where(row == part * chans + chan, last, jnp.zeros_like(last))
            total += dot(table, pair[:, part * count : (part + 1) * count])
    return total


def unpack(data, side, fields):
    chans = fields // 2
    shape = (data.shape[0], data.shape[0] // fields * chans)
    row, chan = iota(shape, 0), iota(shape, 1)
    field = row % fields
    mine = (row // fields * chans + field % chans == chan) & (field // chans == side)
    return contract(data, one_hot(mine), 0, 0)


def slots_of(routes_t, experts):
    count = routes_t.shape[1]
    slots = experts * CAP
    ids = iota((experts, count), 0)
    named = one_hot((routes_t[0:1, :] == ids) | (routes_t[1:2, :] == ids))
    rank = dot(named, one_hot(iota((count, count), 0) < iota((count, count), 1))).astype(bf16)
    spread = one_hot(iota((slots, experts), 0) // CAP == iota((slots, experts), 1))
    slot = (iota((slots, count), 0) % CAP).astype(f32)
    return one_hot((dot(spread, named) > 0.5) & (dot(spread, rank) == slot))


def normalize(x, gain):
    scale = lax.rsqrt(jnp.mean(x * x, axis=-1, keepdims=True) + 1e-05)
    return (x * scale * gain).astype(bf16)


def remote(src, dst, send_sem, recv_sem, **where):
    return pltpu.make_async_remote_copy(
        src_ref=src,
        dst_ref=dst,
        send_sem=send_sem,
        recv_sem=recv_sem,
        device_id=where,
        device_id_type=pl.DeviceIdType.MESH,
    )


class Place:
    def __init__(self, zs=8, xs=4):
        self.zs, self.xs = zs, xs
        self.me = lax.axis_index("ctx")
        self.y = lax.axis_index("ch")
        self.core = self.me % 2
        self.chip = self.me // 2
        self.z = self.chip // xs
        self.x = self.chip % xs
        self.twin = self.me + 1 - 2 * self.core

    def at(self, dz, dx):
        return (self.z + dz + self.zs) % self.zs * self.xs + (self.x + dx + self.xs) % self.xs


def greet(place, count, ys):
    barrier = pltpu.get_barrier_semaphore()

    def tell(**where):
        pl.semaphore_signal(barrier, inc=1, device_id=where, device_id_type=pl.DeviceIdType.MESH)

    tell(ctx=(place.me + count // 2) % count)

    def shard(i, carry):
        tell(ctx=(place.me + count // 2 + i) % count)
        tell(ctx=(place.me + count // 2 - i) % count)
        return carry

    lax.fori_loop(1, count // 2, shard, 0)
    for dy in range(1, ys):
        tell(ch=(place.y + dy) % ys)
    return lambda: pl.semaphore_wait(barrier, count - 1 + ys - 1)


def offsets(q, half, j):
    if half == 0:
        return 4 - q, j
    return (4 + q if q else 0), (j + 1) % 4


def each(q, act):
    for half in range(2):

        def one(j, carry):
            dz, dx = offsets(q, half, j)
            act(q * 8 + half * 4 + j, dz, dx)
            return carry

        lax.fori_loop(0, 3 if q == 0 and half == 1 else 4, one, 0)


def split(refs, counts):
    refs = list(refs)
    return [[refs.pop(0) for _ in range(count)] for count in counts]


def publish_kernel(a_ref, b_ref, a_out, b_out):
    a_out[...] = a_ref[...]
    b_out[...] = b_ref[...]


def layer_kernel(skip, gain, routes_t, *rest):
    place = Place()
    me, core, chip, y = place.me, place.core, place.chip, place.y
    (
        far, (mixed_out, out),
        near, (packed, fields, re_ref, im_ref, conv_out, conv_in, routes_all),
        (send, here, turned, got, summed, back, ups, downs),
        (far_sem, local_sem, conv_sem, xs_sem, xr_sem, send_sem, got_sem, ws_sem, wr_sem, rs_sem, back_sem),
    ) = split(rest, (12, 2, 10, 7, 8, 11))
    shards, width_ch = 64, near[0].shape[1]
    chans = width_ch // shards
    chips, groups, chunk = 32, 4, 8
    ready = greet(place, shards, groups)
    near = (*near, ups.at[0], downs.at[0])
    fetches = [pltpu.make_async_copy(a, b, far_sem.at[i]) for i, (a, b) in enumerate(zip(far, near))]
    for fetch in fetches:
        fetch.start()
    signal, taps, gate, router_t, tables = near[0], near[1], near[2], near[3], near[4:10]
    fetches[0].wait()
    fetches[1].wait()
    packed[...] = pack(signal[...], taps[...], shards, 2 * chans).reshape(packed.shape).astype(bf16)
    routes_all[y] = routes_t[...]
    for fetch in fetches[2:]:
        fetch.wait()
    ready()

    def spread_out(source, target, ss, rs, stay_sem):
        def both(to):
            for side in range(2):
                where = to * 2 + side
                remote(source.at[where], target.at[me], ss, rs, ctx=where).start()

        for q in range(4):
            each(q, lambda slot, dz, dx: both(place.at(dz, dx)))
        remote(source.at[place.twin], target.at[me], ss, rs, ctx=place.twin).start()
        stay = pltpu.make_async_copy(source.at[me], target.at[me], stay_sem)
        stay.start()
        most = pl.ds(0, shards - 1)
        whole = remote(source.at[most], target.at[most], ss, rs, ctx=place.twin)

        def arrive():
            whole.wait_recv()
            stay.wait()

        return whole, arrive

    tells = [
        remote(routes_t, routes_all.at[y], xs_sem.at[dy - 1], xr_sem.at[dy - 1], ch=(y + dy) % groups)
        for dy in range(1, groups)
    ]

    def all_slots():
        for tell in tells:
            tell.wait()
        for k in range(groups):
            here[k] = slots_of(routes_all[k], chips)

    swaps = [
        remote(both.at[0], both.at[1], ws_sem.at[i], wr_sem.at[i], ctx=place.twin)
        for i, both in enumerate((ups, downs))
    ]
    for tell in tells:
        tell.start()
    whole, arrive = spread_out(packed, fields, conv_sem.at[0], conv_sem.at[1], local_sem.at[2])
    all_slots()
    arrive()
    for swap in swaps:
        swap.start()
    data = fields[...].astype(f32).reshape(shards * 2 * chans, -1).astype(bf16)
    product = convolve(data, tables, re_ref, im_ref, shards, chans)
    returns = []
    for side in range(2):
        total = last_step(product, tables, side, shards, chans)
        conv_out[side] = total.reshape(conv_out.shape[1:]).astype(bf16)
        returns.append(
            spread_out(
                conv_out.at[side], conv_in.at[side], conv_sem.at[2 + 2 * side], conv_sem.at[3 + 2 * side],
                local_sem.at[3 + side],
            )
        )
    mine = y * chips + chip
    keep = pltpu.make_async_copy(send.at[mine], got.at[y * chips + 7], local_sem.at[0])
    for side in range(2):
        returns[side][1]()
        data = conv_in[side].astype(f32).reshape(shards * 2 * chans, -1).astype(bf16)
        for part in range(2):
            k = 2 * side + part
            conv = unpack(data, part, 2 * chans)
            count = conv.shape[0]
            span = slice(k * count, (k + 1) * count)
            sig = signal[span, :].astype(f32)
            value = (gate[span, :].astype(f32) * (conv + skip[...] * sig)).astype(bf16)
            mixed_out[span, :] = value
            send[k * chips : (k + 1) * chips] = dot(here[k], value).astype(bf16).reshape(chips, CAP, width_ch)

        for q in (3, 0, 2, 1):

            def dispatch(slot, dz, dx):
                to = place.at(dz, dx)
                for k in range(2 * side, 2 * side + 2):
                    remote(
                        send.at[k * chips + to], got.at[y * chips + slot], send_sem, got_sem.at[q],
                        ctx=to * 2 + core, ch=k,
                    ).start()

            each(q, dispatch)
            for k in range(2 * side, 2 * side + 2) if q == 0 else ():

                @pl.when(y != k)
                def _():
                    remote(
                        send.at[k * chips + chip], got.at[y * chips + 7], send_sem, got_sem.at[0], ch=k
                    ).start()

                pl.when(y == k)(keep.start)

    keep_back = pltpu.make_async_copy(summed.at[y * chips + 7], back.at[mine], local_sem.at[1])
    whole.wait_send()
    for back_half, _ in returns:
        back_half.wait_send()
    for swap in swaps:
        swap.wait()
    column = router_t[pl.ds(chip, 1), :]
    count = here.shape[2]
    turn = one_hot(iota((count, count), 0) == iota((count, count), 1))
    for k in range(groups):
        turned[k] = contract(turn, here[k], 1, 1).astype(bf16)
    for q in (3, 0, 2, 1):
        came = pl.ds(0, groups * chunk - (q == 0))
        remote(send.at[came], got.at[came], send_sem, got_sem.at[q], ctx=me).wait_recv()
        if q == 0:
            keep.wait()
        slices = [got[k * chips + q * chunk : k * chips + (q + 1) * chunk] for k in range(groups)]
        x = jnp.concatenate([piece.reshape(chunk * CAP, width_ch) for piece in slices], axis=1)
        normed = normalize(x.astype(f32), gain[...])
        logit = jnp.sum(normed.astype(f32) * column, axis=-1, keepdims=True)
        total = None
        for half in range(2):
            hidden = jax.nn.gelu(dot(normed, ups[half]), approximate=True).astype(bf16)
            part = dot(hidden, downs[half])
            total = part if half == 0 else total + part
        total = (jax.nn.sigmoid(logit) * total).astype(bf16)
        for k in range(groups):
            piece = total[:, k * width_ch : (k + 1) * width_ch].reshape(chunk, CAP, width_ch)
            summed[k * chips + q * chunk : k * chips + (q + 1) * chunk] = piece

        def give_back(slot, dz, dx):
            to = place.at(-dz, -dx) * 2 + core
            for k in range(groups):
                remote(
                    summed.at[k * chips + slot], back.at[mine], rs_sem, back_sem, ctx=to, ch=k
                ).start()

        each(q, give_back)
        if q == 0:
            for dy in range(1, groups):
                k = (y + dy) % groups
                remote(summed.at[k * chips + 7], back.at[mine], rs_sem, back_sem, ch=k).start()
            keep_back.start()
    keep_back.wait()
    others = pl.ds(0, groups * chips - 1)
    remote(summed.at[others], back.at[others], rs_sem, back_sem, ctx=me).wait_recv()
    for k in range(groups):
        slots = back[k * chips : (k + 1) * chips].reshape(chips * CAP, width_ch)
        rows = dot(turned[k], slots).astype(bf16)
        out[k * rows.shape[0] : (k + 1) * rows.shape[0], :] = rows
    remote(send.at[others], got.at[others], send_sem, got_sem.at[0], ctx=me).wait_send()
    remote(summed.at[others], back.at[others], rs_sem, back_sem, ctx=me).wait_send()


def body(signal, gate_v, taps, skip, norm_gain, router, w_up, w_down, routes):
    tok_dev, ch_dev = signal.shape
    shards = lax.axis_size("ctx")
    groups = lax.axis_size("ch")
    chans = ch_dev // shards
    experts = router.shape[1]
    width = norm_gain.shape[0]
    rows = tok_dev // groups
    shape = jax.ShapeDtypeStruct
    far = (
        signal, taps, gate_v, router.T, *dft_constants(shards, tok_dev, chans), w_up[0], w_down[0],
    )
    hidden = w_up.shape[2]
    blocks = (groups * experts, CAP, ch_dev)
    dma = pltpu.SemaphoreType.DMA
    vmem = pltpu.VMEM
    here = pl.BlockSpec(memory_space=vmem)
    there = pl.BlockSpec(memory_space=pl.ANY)
    local = shape((tok_dev, ch_dev), bf16)
    results = pl.pallas_call(
        layer_kernel,
        out_shape=(local, local),
        in_specs=[here] * 3 + [there] * len(far),
        out_specs=(here, here),
        scratch_shapes=[vmem(a.shape, a.dtype) for a in far[:-2]]
        + [vmem((shards, 2 * chans, tok_dev), bf16)] * 2
        + [vmem((2 * chans * shards, tok_dev), bf16)] * 2
        + [vmem((2, shards, 2 * chans, tok_dev // 4), bf16)] * 2
        + [vmem((groups, 2, rows), routes.dtype)]
        + [vmem(blocks, bf16)]
        + [vmem((groups, experts * CAP, rows), bf16), vmem((groups, rows, experts * CAP), bf16)]
        + [vmem(blocks, bf16)] * 3
        + [vmem((2, width, hidden), bf16), vmem((2, hidden, width), bf16)]
        + [dma((12,)), dma((5,)), dma((6,)), dma((3,)), dma((3,)), dma]
        + [dma((4,)), dma((2,)), dma((2,)), dma, dma],
        compiler_params=pltpu.CompilerParams(collective_id=0, has_side_effects=True),
    )(skip[None, :], norm_gain[None, :], routes.T, *far)
    return tuple(
        pl.pallas_call(
            publish_kernel,
            out_shape=(local, local),
            in_specs=[here] * 2,
            out_specs=(here, here),
        )(*results)
    )


def solution(mesh):
    in_specs = (
        P("ctx", "ch"),
        P("ctx", "ch"),
        P("ctx", "ch"),
        P("ch"),
        P(),
        P(),
        P("ctx", None, None),
        P("ctx", None, None),
        P(("ctx", "ch"), None),
    )
    out_specs = (P("ctx", "ch"), P("ctx", "ch"))
    return jax.shard_map(body, mesh=mesh, in_specs=in_specs, out_specs=out_specs, check_vma=False)
```
